128 devices in a mesh: child: 4 (over y), tile: 32 (over x, z, core).
Axes of the slice: x: 4, y: 4, z: 4, core: 2. Of those that a mesh axis runs over, the one named last changes fastest.
Arguments:
- child_tiles: bfloat16 [4, 512, 512, 512], P('child', 'tile'), may hold values from -6 to 6
- panel: bfloat16 [4, 16384, 512], P('child', 'tile'), may hold values from -1 to 1
- bases: bfloat16 [4, 16384, 128], P('child', 'tile'), may hold values from -0.25 to 0.25
- tile_blocks: int32 [4, 512, 2], P('child'), may hold values from 0 to 31, as said below
- tile_dest: int32 [4, 512, 1], P('child'), may hold values from 0 to 31; in each aligned block of 16 rows (0 to 15, 16 to 31, ..., all dimensions but the last counted through in order) at most 2 rows name the same one
- tile_slot: int32 [4, 512], P('child'), may hold values from 0 to 7
- parent_tiles: bfloat16 [4, 256, 512, 512], P('child', 'tile'), may hold values from -6 to 6
- parent_blocks: int32 [4, 256, 2], P('child', 'tile'), may hold values from 0 to 31, as said below
- sketch_test: bfloat16 [16384, 128], replicated, may hold values from -0.25 to 0.25
Outputs:
- updated_tiles: bfloat16 [4, 256, 512, 512], P('child', 'tile')
- row_sketch: float32 [16384, 128], P(('child', 'tile'))
The draws below stay inside these ranges and needn't reach their ends.
Inputs may be any that keep to these rules, and one draw needn't show every extreme that they name: `tile_blocks`: each tile's row block is not below its column block. `tile_dest`: among the tiles of one device (aligned blocks of 16 tiles of a child), at most 2 name the same owner. `parent_blocks`: each parent tile's row block is not below its column block.
All inputs are finite; a program needn't handle non-finite values.
Results may differ from the reference program's by a relative error of at most 0.0063.
Values may be sent and summed in bfloat16 or wider, within the bound.
A program may use at most 192 MiB of HBM per device.

```python
import math
import jax
import jax.numpy as jnp
import numpy as np
from jax import lax

TILE = 512
RANK = 128
SKETCH = 128
TILES_DEV = 16
PARENT_DEV = 8
CAP = 2
BLOCKS = 32
PBLOCKS = 32
TILES = 512
PTILES = 256
N_CHILD = 4
N_TILE = 32


def draw_tile_blocks(key, part):
    first_key, second_key = jax.random.split(jax.random.fold_in(key, 11))
    row_ids = jax.random.randint(first_key, (N_CHILD, TILES, 1), 0, BLOCKS)
    col_ids = jax.random.randint(second_key, (N_CHILD, TILES, 1), 0, row_ids + 1)
    return jnp.concatenate([row_ids, col_ids], axis=2).astype(jnp.int32)


def draw_parent_blocks(key, part):
    first_key, second_key = jax.random.split(jax.random.fold_in(key, 23))
    row_ids = jax.random.randint(first_key, (N_CHILD, PTILES, 1), 0, PBLOCKS)
    col_ids = jax.random.randint(second_key, (N_CHILD, PTILES, 1), 0, row_ids + 1)
    return jnp.concatenate([row_ids, col_ids], axis=2).astype(jnp.int32)


def plant(values, rng, low, top_value):
    longest = values.shape.index(max(values.shape))
    spots = []
    for shift in (0, 1):
        where = [jax.random.randint(jax.random.fold_in(rng, axis), (), 0, length) for axis, length in enumerate(values.shape)]
        where[longest] = (where[longest] + shift) % values.shape[longest]
        spots.append(tuple(where))
    return values.at[spots[0]].set(low).at[spots[1]].set(top_value)


def shard_levels(stream_key, shape, shards, smallest, largest):
    def one(position, blocks):
        draws = jax.random.uniform(jax.random.fold_in(jax.random.fold_in(stream_key, 6), position), (blocks,), jnp.float32, smallest / len(shards), largest / len(shards))
        return jnp.repeat(jnp.exp(draws), shape[position] // blocks).reshape((-1,) + (1,) * (len(shape) - position - 1))

    factor_of = one(*shards[0])
    for cut in shards[1:]:
        factor_of = factor_of * one(*cut)
    return factor_of


def routed_block(rng, own, number, rows, count, top, bound, skew):
    sequence = jax.random.permutation(rng, count)
    heavy_load, common = shares(count, rows * top, bound, skew, True), shares(count, rows * top, bound, skew, False)
    places = jnp.arange(count)

    def named(sizes, turn):
        used = int((sizes > 0).sum())
        fixed = max(1, used // 4)
        passed = fixed + (places - fixed + turn * (used - fixed)) % max(1, count - fixed)
        return jnp.zeros((count,), jnp.int32).at[sequence[jnp.where(places < fixed, places, passed)]].set(jnp.asarray(sizes, jnp.int32))

    sizes = jnp.where(number % 4 == 0, named(heavy_load, number // 4), named(common, number - number // 4 - 1))
    mixed = jax.random.permutation(jax.random.fold_in(own, 3), count)
    source_of, taker = mixed[0:count // 2 * 2:2], mixed[1:count // 2 * 2:2]
    room = jnp.minimum(sizes[source_of] - 1, bound - sizes[taker]) // 2
    room = jnp.where((source_of == sequence[0]) | (taker == sequence[0]) | (sizes[taker] == 0), 0, jnp.maximum(room, 0))
    passed = jax.random.randint(jax.random.fold_in(own, 4), (count // 2,), 0, 1 << 20) % (room + 1)
    sizes = sizes.at[source_of].add(-passed).at[taker].add(passed)
    labels = jnp.searchsorted(jnp.cumsum(sizes), jnp.arange(rows * top), side="right").astype(jnp.int32)
    grid = labels.reshape(top, rows).T
    grid = grid[jax.random.permutation(jax.random.fold_in(own, 1), rows)]
    turn = jax.random.randint(jax.random.fold_in(own, 2), (rows, 1), 0, top)
    return jnp.take_along_axis(grid, (jnp.arange(top)[None, :] + turn) % top, axis=1)


def shares(number_of, total, bound, slope, full):
    loads = [(1 << 20) // math.isqrt(rank ** slope) + 1 for rank in range(1, number_of + 1)]
    largest = bound if full else min(bound, max(-(-total // number_of), total * loads[0] // sum(loads)))
    least = 1 if total - largest >= number_of - 1 else 0
    given, rest = [largest] + [least] * (number_of - 1), total - largest - least * (number_of - 1)
    while rest > 0:
        candidates = [i for i in range(1, number_of) if given[i] < largest] or [i for i in range(1, number_of) if given[i] < bound]
        mass, budget = sum([loads[i] for i in candidates]), rest
        for i in candidates:
            addition = min(bound - given[i], max(1, budget * loads[i] // mass), rest)
            given[i] = given[i] + addition
            rest = rest - addition
    return np.array(given)


def normal_values(own_key, dims, deviation, reach, shards=(), dtype=jnp.bfloat16):
    level = shard_levels(own_key, dims, shards, -0.22, 0.18) if shards else 1.0
    result = jax.random.normal(own_key, dims, jnp.float32) * deviation * level
    return jnp.minimum(jnp.maximum(result, -reach), reach).astype(dtype)


def setup_inputs(seed: int = 0) -> dict:
    key_of = jax.random.split(jax.random.key(seed), 10)
    child_tiles = normal_values(key_of[0], (N_CHILD, TILES, TILE, TILE), 1.0, 6.0, ((0, 4), (1, 32)))
    panel = normal_values(key_of[1], (N_CHILD, BLOCKS * TILE, TILE), 0.21, 1.0, ((0, 4), (1, 32)))
    bases = normal_values(key_of[2], (N_CHILD, BLOCKS * TILE, RANK), TILE ** -0.5, 0.25, ((0, 4), (1, 32)))
    tile_blocks = draw_tile_blocks(jax.random.fold_in(key_of[9], 71), 0)
    tile_dest_keys = jax.random.split(jax.random.fold_in(key_of[4], 1), N_CHILD * TILES // TILES_DEV)
    tile_dest_turns = jax.random.permutation(jax.random.fold_in(key_of[4], 3), N_CHILD * TILES // TILES_DEV)
    tile_dest = jax.vmap(lambda own, number: routed_block(jax.random.fold_in(key_of[4], 2), own, number, TILES_DEV, N_TILE, 1, CAP, 2))(tile_dest_keys, tile_dest_turns).reshape((N_CHILD, TILES, 1))
    tile_slot = plant(jax.random.randint(key_of[5], (N_CHILD, TILES), 0, PARENT_DEV), jax.random.fold_in(key_of[5], 1), 0, PARENT_DEV - 1).astype(jnp.int32)
    parent_tiles = normal_values(key_of[6], (N_CHILD, PTILES, TILE, TILE), 1.0, 6.0, ((0, 4), (1, 32)))
    parent_blocks = draw_parent_blocks(jax.random.fold_in(key_of[9], 71), 0)
    sketch_test = normal_values(key_of[8], (PBLOCKS * TILE, SKETCH), TILE ** -0.5, 0.25)
    return {"child_tiles": child_tiles, "panel": panel, "bases": bases, "tile_blocks": tile_blocks, "tile_dest": tile_dest, "tile_slot": tile_slot, "parent_tiles": parent_tiles, "parent_blocks": parent_blocks, "sketch_test": sketch_test}


def reference(child_tiles, panel, bases, tile_blocks, tile_dest, tile_slot, parent_tiles, parent_blocks, sketch_test):
    test_blocks = sketch_test.reshape(PBLOCKS, TILE, SKETCH)
    sketch_acc = jnp.zeros((PBLOCKS, TILE, SKETCH), jnp.float32)
    results = []
    for child_id in range(N_CHILD):
        panel_blocks = panel[child_id].reshape(BLOCKS, TILE, TILE)
        basis_blocks = bases[child_id].reshape(BLOCKS, TILE, RANK)
        panel_proj = jnp.einsum("bxr,bxy->bry", basis_blocks.astype(jnp.float32), panel_blocks.astype(jnp.float32)).astype(jnp.bfloat16)
        targets = (tile_dest[child_id, :, 0] * PARENT_DEV + tile_slot[child_id]).astype(jnp.int32)

        def advance(summed, pieces):
            tile_block, row_id, col_id, target = pieces
            left_basis = basis_blocks[row_id]
            right_basis = basis_blocks[col_id]
            half = jnp.dot(left_basis.T, tile_block, preferred_element_type=jnp.float32).astype(jnp.bfloat16)
            encoded = jnp.dot(half, right_basis, preferred_element_type=jnp.float32)
            cross = jnp.dot(panel_proj[row_id], panel_proj[col_id].T, preferred_element_type=jnp.float32)
            core = (encoded - cross).astype(jnp.bfloat16)
            left_part = jnp.dot(left_basis, core, preferred_element_type=jnp.float32).astype(jnp.bfloat16)
            decoded = jnp.dot(left_part, right_basis.T, preferred_element_type=jnp.float32)
            return summed.at[target].add(decoded), None

        summed, _ = lax.scan(advance, parent_tiles[child_id].astype(jnp.float32),
                             (child_tiles[child_id], tile_blocks[child_id, :, 0], tile_blocks[child_id, :, 1], targets))
        updated = summed.astype(jnp.bfloat16)
        results.append(updated)

        def sketch_step(accum, pieces):
            parent_block, prow, pcol = pieces
            direct = jnp.dot(parent_block, test_blocks[pcol], preferred_element_type=jnp.float32)
            second = jnp.dot(parent_block.T, test_blocks[prow], preferred_element_type=jnp.float32)
            second = second * (prow != pcol).astype(jnp.float32)
            accum = accum.at[prow].add(direct)
            accum = accum.at[pcol].add(second)
            return accum, None

        sketch_acc, _ = lax.scan(sketch_step, sketch_acc, (updated, parent_blocks[child_id, :, 0], parent_blocks[child_id, :, 1]))
    return jnp.stack(results, axis=0), sketch_acc.reshape(PBLOCKS * TILE, SKETCH)
```

```python
import functools

import jax
import jax.numpy as jnp
from jax import lax
from jax.experimental import pallas as pl
from jax.experimental.pallas import tpu as pltpu
from jax.sharding import PartitionSpec as P

CAP = 2
SIDE = 4
F32 = jnp.float32
BF16 = jnp.bfloat16
SPLIT = ((0, 48), (48, 48), (96, 32))
ORDERS = ((0, 1, 2), (1, 2, 0), (2, 0, 1))


def dot(a, b, ca, cb):
    return lax.dot_general(a, b, (((ca,), (cb,)), ((), ())), preferred_element_type=F32)


def shift(p, by):
    return lax.rem(p + by + SIDE, SIDE)


def greet(devices):
    barrier = pltpu.get_barrier_semaphore()
    for device in devices:
        pl.semaphore_signal(barrier, inc=1, device_id=device)


def await_greetings(count):
    pl.semaphore_wait(pltpu.get_barrier_semaphore(), count)


def route_kernel(
    owners,
    idx_ref,
    panel_hbm,
    bases_hbm,
    tiles_hbm,
    bases_out,
    cores_out,
    table_ref,
    tiles,
    panel,
    bases,
    proj,
    cores,
    outgoing,
    load_sem,
    own_sem,
    send_sem,
    recv_sem,
    a2a_send,
    a2a_recv,
):
    t = lax.axis_index("tile")
    x, z, c = t // 8, lax.rem(t // 2, SIDE), lax.rem(t, 2)
    count = tiles.shape[0]

    load_panel = pltpu.make_async_copy(panel_hbm, panel, load_sem.at[0])
    load_bases = pltpu.make_async_copy(bases_hbm, bases.at[t], load_sem.at[1])
    load_tiles = pltpu.make_async_copy(tiles_hbm, tiles, load_sem.at[2])
    load_panel.start()
    load_bases.start()
    load_tiles.start()

    @pl.loop(1, owners)
    def _(step):
        pl.semaphore_signal(
            pltpu.get_barrier_semaphore(),
            inc=1,
            device_id={"tile": lax.rem(t + step, owners)},
        )

    load_panel.wait()
    load_bases.wait()
    proj[t] = dot(bases[t], panel[...], 0, 0).astype(BF16)
    await_greetings(owners - 1)

    def along_x(first, second):
        return first * 8 + second * 2 + c

    def along_z(first, second):
        return second * 8 + first * 2 + c

    sibling = t + 1 - 2 * c
    pending = []

    class Gather:
        def __init__(self, buf, number, first, second, device):
            self.buf, self.n, self.f, self.s, self.dev = buf, number, first, second, device
            self.half = buf.shape[1] // 2

        def copy(self, block, half, peer, k):
            ref = self.buf.at[block]
            if half is not None:
                ref = ref.at[pl.ds(half * self.half, self.half)]
            return pltpu.make_async_remote_copy(
                src_ref=ref,
                dst_ref=ref,
                send_sem=send_sem.at[self.n, k],
                recv_sem=recv_sem.at[self.n, k],
                device_id={"tile": peer},
            )

        def send(self, block, half, peer, k):
            copy = self.copy(block, half, peer, k)
            copy.start()
            pending.append(copy)

        def to_sibling(self, block, k):
            self.send(block, None, sibling, 20 + k)

        def open_ring(self, ring, place):
            block, up, down = place(0), place(1, True), place(-1, True)
            self.send(block, None, up, 4 * ring)
            self.send(block, None, down, 4 * ring + 1)

        def relay_up(self, ring, place):
            block = place(-1)
            self.copy(block, None, place(-1, True), 4 * ring).wait_recv()
            self.send(block, 0, place(1, True), 4 * ring + 2)
            return block

        def relay_down(self, ring, place):
            block = place(1)
            self.copy(block, None, place(1, True), 4 * ring + 1).wait_recv()
            self.send(block, 1, place(-1, True), 4 * ring + 3)
            return block

        def close_ring(self, ring, place):
            block = place(2)
            self.copy(block, 0, place(-1, True), 4 * ring + 2).wait_recv()
            self.copy(block, 1, place(1, True), 4 * ring + 3).wait_recv()
            return block

        def first_ring(self):
            def place(by, device=False):
                return self.dev(shift(self.f, by), self.s)

            return place

        def second_ring(self, offset):
            def place(by, device=False):
                first = self.f if device else shift(self.f, offset)
                return self.dev(first, shift(self.s, by))

            return place

    both = (Gather(bases, 0, x, z, along_x), Gather(proj, 1, z, x, along_z))
    offsets = (None, 0, -1, 1, 2)
    seconds = [[g.second_ring(o) if o is not None else None for o in offsets] for g in both]
    for g, s in zip(both, seconds):
        g.open_ring(0, g.first_ring())
        g.open_ring(1, s[1])
        g.to_sibling(t, 0)
    for g, s in zip(both, seconds):
        g.to_sibling(g.relay_up(0, g.first_ring()), 1)
        g.open_ring(2, s[2])
        g.to_sibling(g.relay_down(0, g.first_ring()), 2)
        g.open_ring(3, s[3])
    for g, s in zip(both, seconds):
        g.to_sibling(g.relay_up(1, s[1]), 3)
        g.to_sibling(g.relay_down(1, s[1]), 4)
    for g, s in zip(both, seconds):
        g.to_sibling(g.close_ring(0, g.first_ring()), 5)
        g.open_ring(4, s[4])
    for ring in (2, 3):
        for g, s in zip(both, seconds):
            g.to_sibling(g.relay_up(ring, s[ring]), 2 * ring + 2)
            g.to_sibling(g.relay_down(ring, s[ring]), 2 * ring + 3)
    for g, s in zip(both, seconds):
        g.to_sibling(g.close_ring(1, s[1]), 10)
    for g, s in zip(both, seconds):
        g.to_sibling(g.relay_up(4, s[4]), 11)
        g.to_sibling(g.relay_down(4, s[4]), 12)
    for ring in (2, 3, 4):
        for g, s in zip(both, seconds):
            g.to_sibling(g.close_ring(ring, s[ring]), 11 + ring)
    for g, s in zip(both, seconds):
        first = g.first_ring()
        order = [
            first(0), first(-1), first(1), s[1](-1), s[1](1), first(2),
            s[2](-1), s[2](1), s[3](-1), s[3](1), s[1](2), s[4](-1), s[4](1),
            s[2](2), s[3](2), s[4](2),
        ]
        for k, block in enumerate(order):
            g.copy(block + 1 - 2 * c, None, sibling, 20 + k).wait_recv()
    for copy in pending:
        copy.wait_send()

    keep_bases = pltpu.make_async_copy(bases, bases_out, own_sem.at[0])
    keep_bases.start()
    load_tiles.wait()

    @pl.loop(0, count)
    def _(q):
        entry = idx_ref[t * count + q]
        i, j = entry & 255, (entry >> 8) & 255
        half = dot(bases[i], tiles[q], 0, 0).astype(BF16)
        core = dot(half, bases[j], 1, 0) - dot(proj[i], proj[j], 1, 1)
        cores[q] = core.astype(BF16)

    dests = [idx_ref[t * count + q] >> 24 for q in range(count)]

    def outbound(step, target):
        return pltpu.make_async_remote_copy(
            src_ref=outgoing.at[step],
            dst_ref=cores_out.at[t],
            send_sem=a2a_send.at[step],
            recv_sem=a2a_recv.at[step],
            device_id={"tile": target},
        )

    def pack(step, target):
        first, last = jnp.int32(0), jnp.int32(0)
        for q in range(count):
            last = jnp.where(dests[q] == target, q, last)
            back = count - 1 - q
            first = jnp.where(dests[back] == target, back, first)
        outgoing[step, 0] = cores[first]
        outgoing[step, 1] = cores[last]

    @pl.loop(1, owners)
    def _(step):
        target = lax.rem(t + step, owners)
        pack(step, target)
        outbound(step, target).start()

    pack(0, t)
    keep_own = pltpu.make_async_copy(outgoing.at[0], cores_out.at[t], own_sem.at[1])
    keep_own.start()

    @pl.loop(0, owners)
    def _(source):
        first, last, found = jnp.int32(0), jnp.int32(0), jnp.int32(0)
        for q in range(count):
            entry = idx_ref[source * count + q]
            hit = (entry >> 24) == t
            last = jnp.where(hit, entry, last)
            first = jnp.where(hit & (found == 0), entry, first)
            found = found + hit.astype(jnp.int32)
        table_ref[source * CAP] = jnp.where(found > 0, first, -1)
        table_ref[source * CAP + 1] = jnp.where(found > 1, last, -1)

    @pl.loop(1, owners)
    def _(step):
        source = lax.rem(t - step + owners, owners)
        pltpu.make_async_remote_copy(
            src_ref=outgoing.at[step],
            dst_ref=cores_out.at[source],
            send_sem=a2a_send.at[step],
            recv_sem=a2a_recv.at[step],
            device_id={"tile": source},
        ).wait()

    keep_own.wait()
    keep_bases.wait()


def decode_kernel(
    table_ref,
    pblocks_ref,
    bases_hbm,
    cores_hbm,
    parents_hbm,
    test_hbm,
    updated_hbm,
    sketch_hbm,
    bases,
    cores,
    parents,
    test,
    total,
    part,
    rounded,
    load_sem,
    tile_sem,
    store_sem,
):
    held = parents.shape[0]
    blocks = part.shape[0]
    loads = [
        pltpu.make_async_copy(bases_hbm, bases, load_sem.at[0]),
        pltpu.make_async_copy(cores_hbm, cores, load_sem.at[1]),
    ]
    tiles = [
        pltpu.make_async_copy(parents_hbm.at[p], parents.at[p], tile_sem.at[p])
        for p in range(held)
    ]
    load_test = pltpu.make_async_copy(test_hbm, test, load_sem.at[2])
    for copy in tiles + loads + [load_test]:
        copy.start()

    @pl.loop(0, blocks)
    def _(b):
        part[b] = jnp.zeros_like(part[b])

    for p in range(held):
        tiles[p].wait()
        total[p] = parents[p].astype(F32)
    for copy in loads:
        copy.wait()

    @pl.loop(0, cores.shape[0])
    def _(k):
        entry = table_ref[k]

        @pl.when(entry >= 0)
        def _():
            i, j, slot = entry & 255, (entry >> 8) & 255, (entry >> 16) & 255
            left = dot(bases[i], cores[k], 1, 0).astype(BF16)
            total[slot] += dot(left, bases[j], 1, 1)

    load_test.wait()
    stores = []
    for p in range(held):
        a, b = pblocks_ref[2 * p], pblocks_ref[2 * p + 1]
        new = total[p].astype(BF16)
        parents[p] = new
        store = pltpu.make_async_copy(parents.at[p], updated_hbm.at[p], tile_sem.at[p])
        store.start()
        stores.append(store)
        part[a] += dot(new, test[b], 1, 0)

        @pl.when(a != b)
        def _():
            part[b] += dot(new, test[a], 0, 0)

    groups = 4
    size = blocks // groups
    for g in range(groups):
        span = pl.ds(g * size, size)
        rounded[span] = part[span].astype(BF16)
        store = pltpu.make_async_copy(rounded.at[span], sketch_hbm.at[span], store_sem.at[g])
        store.start()
        stores.append(store)
    for store in stores:
        store.wait()


def reduce_kernel(part_hbm, out_ref, *scratch):
    n = len(SPLIT)
    mine, heard, held = scratch[:n], scratch[n : 2 * n], scratch[2 * n : 3 * n]
    got1, held2, got2, held3, got3 = (scratch[(3 + i) * n : (4 + i) * n] for i in range(5))
    own_sem, send_sem, recv_sem = scratch[8 * n :]
    y, t = lax.axis_index("child"), lax.axis_index("tile")
    x, z, c = t // 8, lax.rem(t // 2, SIDE), lax.rem(t, 2)
    here = (y, x, z)

    def device(coords, core):
        return {"child": coords[0], "tile": coords[1] * 8 + coords[2] * 2 + core}

    def moved(axis, by):
        return tuple(shift(p, by) if a == axis else p for a, p in enumerate(here))

    sibling = device(here, 1 - c)
    greet([sibling] + [device(moved(a, by), c) for a in range(3) for by in (1, 2, 3)])

    own = []
    for k, (at, rows) in enumerate(SPLIT):
        copy = pltpu.make_async_copy(
            part_hbm.at[:, :, :, c, pl.ds(at, rows)], mine[k], own_sem.at[k]
        )
        copy.start()
        own.append(copy)
    await_greetings(10)

    pending = []

    def remote(src, dst, number, peer):
        copy = pltpu.make_async_remote_copy(
            src_ref=src,
            dst_ref=dst,
            send_sem=send_sem.at[number],
            recv_sem=recv_sem.at[number],
            device_id=peer,
        )
        pending.append(copy)
        copy.start()
        return copy

    swaps = [
        remote(part_hbm.at[:, :, :, 1 - c, pl.ds(at, rows)], heard[k], 30 + k, sibling)
        for k, (at, rows) in enumerate(SPLIT)
    ]

    def pick(ref, axis, which):
        return ref.at[(slice(None),) * axis + (which,)]

    def left_axes(k, stage):
        axes = [a for a in range(3) if a not in ORDERS[k][:stage]]
        return axes.index(ORDERS[k][stage])

    def scatter(k, stage, buf, got):
        axis, copies = ORDERS[k][stage], []
        at = left_axes(k, stage)
        for by in (1, 3, 2):
            copies.append(
                remote(
                    pick(buf, at, shift(here[axis], by)),
                    got.at[by - 1],
                    9 * k + 3 * stage + by - 1,
                    device(moved(axis, by), c),
                )
            )
        return copies

    def gather_up(k, stage, buf, got, copies, dst):
        axis = ORDERS[k][stage]
        for copy in copies:
            copy.wait_recv()
        kept = pick(buf, left_axes(k, stage), here[axis])[...].astype(F32)
        value = kept + got[0].astype(F32) + got[1].astype(F32) + got[2].astype(F32)
        dst[...] = value.astype(dst.dtype)

    flying = []
    for k in range(n):
        own[k].wait()
        swaps[k].wait_recv()

        @pl.loop(0, SIDE)
        def _(a):
            held[k][a] = (mine[k][a].astype(F32) + heard[k][a].astype(F32)).astype(BF16)

        flying.append(scatter(k, 0, held[k], got1[k]))
    for k in range(n):
        gather_up(k, 0, held[k], got1[k], flying[k], held2[k])
        flying[k] = scatter(k, 1, held2[k], got2[k])
    for k in range(n):
        gather_up(k, 1, held2[k], got2[k], flying[k], held3[k])
        flying[k] = scatter(k, 2, held3[k], got3[k])
    for k, (at, rows) in enumerate(SPLIT):
        gather_up(k, 2, held3[k], got3[k], flying[k], out_ref.at[pl.ds(at, rows)])
    for copy in pending:
        copy.wait_send()


def shards(
    child_tiles,
    panel,
    bases,
    tile_blocks,
    tile_dest,
    tile_slot,
    parent_tiles,
    parent_blocks,
    sketch_test,
):
    owners = lax.axis_size("tile")
    _, count, order, _ = child_tiles.shape
    rank = bases.shape[2]
    width = sketch_test.shape[1]
    held = parent_tiles.shape[1]
    blocks = sketch_test.shape[0] // order
    chunk = sketch_test.shape[0] // (SIDE**3 * 2)
    any_space = pl.BlockSpec(memory_space=pl.ANY)
    smem = pl.BlockSpec(memory_space=pltpu.SMEM)
    vmem = pl.BlockSpec(memory_space=pltpu.VMEM)
    dma = pltpu.SemaphoreType.DMA

    packed = (
        tile_blocks[0, :, 0]
        + tile_blocks[0, :, 1] * 256
        + tile_slot[0] * 65536
        + tile_dest[0, :, 0] * 16777216
    )
    whole_bases, cores, table = pl.pallas_call(
        functools.partial(route_kernel, owners),
        out_shape=(
            jax.ShapeDtypeStruct((owners, order, rank), BF16),
            jax.ShapeDtypeStruct((owners, CAP, rank, rank), BF16),
            jax.ShapeDtypeStruct((owners * CAP,), jnp.int32),
        ),
        in_specs=[smem, any_space, any_space, any_space],
        out_specs=(any_space, any_space, smem),
        scratch_shapes=[
            pltpu.VMEM((count, order, order), BF16),
            pltpu.VMEM((order, order), BF16),
            pltpu.VMEM((owners, order, rank), BF16),
            pltpu.VMEM((owners, rank, order), BF16),
            pltpu.VMEM((count, rank, rank), BF16),
            pltpu.VMEM((owners, CAP, rank, rank), BF16),
            dma((3,)),
            dma((2,)),
            dma((2, 36)),
            dma((2, 36)),
            dma((owners,)),
            dma((owners,)),
        ],
        compiler_params=pltpu.CompilerParams(
            collective_id=0, has_side_effects=True, vmem_limit_bytes=40 << 20
        ),
        name="encode_and_route",
    )(packed, panel[0], bases[0], child_tiles[0])

    updated, part = pl.pallas_call(
        decode_kernel,
        out_shape=(
            jax.ShapeDtypeStruct((held, order, order), BF16),
            jax.ShapeDtypeStruct((blocks, order, width), BF16),
        ),
        in_specs=[smem, smem, any_space, any_space, any_space, any_space],
        out_specs=(any_space, any_space),
        scratch_shapes=[
            pltpu.VMEM((owners, order, rank), BF16),
            pltpu.VMEM((owners * CAP, rank, rank), BF16),
            pltpu.VMEM((held, order, order), BF16),
            pltpu.VMEM((blocks, order, width), BF16),
            pltpu.VMEM((held, order, order), F32),
            pltpu.VMEM((blocks, order, width), F32),
            pltpu.VMEM((blocks, order, width), BF16),
            dma((3,)),
            dma((held,)),
            dma((4,)),
        ],
        compiler_params=pltpu.CompilerParams(vmem_limit_bytes=52 << 20),
        name="decode_and_sketch",
    )(
        table,
        parent_blocks.reshape(-1),
        whole_bases,
        cores.reshape(owners * CAP, rank, rank),
        parent_tiles[0],
        sketch_test.reshape(blocks, order, width),
    )

    def bufs(*lead):
        return [pltpu.VMEM((*lead, rows, width), BF16) for _, rows in SPLIT]

    row_sketch = pl.pallas_call(
        reduce_kernel,
        out_shape=jax.ShapeDtypeStruct((chunk, width), F32),
        in_specs=[any_space],
        out_specs=vmem,
        scratch_shapes=[
            *bufs(4, 4, 4),
            *bufs(4, 4, 4),
            *bufs(4, 4, 4),
            *bufs(3, 4, 4),
            *bufs(4, 4),
            *bufs(3, 4),
            *bufs(4),
            *bufs(3),
            dma((3,)),
            dma((33,)),
            dma((33,)),
        ],
        compiler_params=pltpu.CompilerParams(
            collective_id=1, has_side_effects=True, vmem_limit_bytes=32 << 20
        ),
        name="reduce_sketch",
    )(part.reshape(SIDE, SIDE, SIDE, 2, chunk, width))
    return (updated[None], row_sketch)


def solution(mesh):
    return jax.shard_map(
        shards,
        mesh=mesh,
        in_specs=(
            P("child", "tile", None, None),
            P("child", "tile", None),
            P("child", "tile", None),
            P("child", None, None),
            P("child", None, None),
            P("child", None),
            P("child", "tile", None, None),
            P("child", "tile", None),
            P(),
        ),
        out_specs=(P("child", "tile", None, None), P(("child", "tile"), None)),
        check_vma=False,
    )
```

```python
import functools

import jax
import jax.numpy as jnp
from jax import lax
from jax.experimental import pallas as pl
from jax.experimental.pallas import tpu as pltpu
from jax.sharding import PartitionSpec as P

CAP = 2
SIDE = 4
F32 = jnp.float32
BF16 = jnp.bfloat16
SPLIT = ((0, 48), (48, 48), (96, 32))
ORDERS = ((0, 1, 2), (1, 2, 0), (2, 0, 1))


def dot(a, b, ca, cb):
    return lax.dot_general(a, b, (((ca,), (cb,)), ((), ())), preferred_element_type=F32)


def shift(p, by):
    return lax.rem(p + by + SIDE, SIDE)


def greet(devices):
    barrier = pltpu.get_barrier_semaphore()
    for device in devices:
        pl.semaphore_signal(barrier, inc=1, device_id=device)


def await_greetings(count):
    pl.semaphore_wait(pltpu.get_barrier_semaphore(), count)


def route_kernel(
    owners,
    blocks_ref,
    dest_ref,
    slot_ref,
    panel_hbm,
    bases_hbm,
    tiles_hbm,
    bases_out,
    cores_out,
    table_ref,
    tiles,
    panel,
    bases,
    proj,
    encoded,
    cores,
    outgoing,
    load_sem,
    own_sem,
    send_sem,
    recv_sem,
    a2a_send,
    a2a_recv,
):
    t = lax.axis_index("tile")
    x, z, c = t // 8, lax.rem(t // 2, SIDE), lax.rem(t, 2)
    count = tiles.shape[0]

    load_panel = pltpu.make_async_copy(panel_hbm, panel, load_sem.at[0])
    load_bases = pltpu.make_async_copy(bases_hbm, bases.at[x, z, c], load_sem.at[1])
    load_tiles = pltpu.make_async_copy(tiles_hbm, tiles, load_sem.at[2])
    load_bases.start()
    load_panel.start()
    load_tiles.start()

    @pl.loop(1, owners)
    def _(step):
        pl.semaphore_signal(
            pltpu.get_barrier_semaphore(),
            inc=1,
            device_id={"tile": lax.rem(t + step, owners)},
        )

    load_bases.wait()
    load_panel.wait()
    proj[x, z, c] = dot(bases[x, z, c], panel[...], 0, 0).astype(BF16)
    await_greetings(owners - 1)

    sibling = t + 1 - 2 * c
    pending = []

    class Gather:
        offsets = (None, 0, -1, 1, 2)

        def __init__(self, number, buf, x_first):
            self.n, self.buf, self.x_first = number, buf, x_first
            self.f, self.s = (x, z) if x_first else (z, x)
            self.rows = buf.shape[3]

        def at(self, first, second, core):
            return self.buf.at[(first, second, core) if self.x_first else (second, first, core)]

        def place(self, ring, by):
            if ring == 0:
                return shift(self.f, by), self.s
            return shift(self.f, self.offsets[ring]), shift(self.s, by)

        def peer(self, ring, by):
            first, second = (self.f, shift(self.s, by)) if ring else self.place(0, by)
            return (first if self.x_first else second) * 8 + (second if self.x_first else first) * 2 + c

        def copy(self, ref, peer, k):
            return pltpu.make_async_remote_copy(
                src_ref=ref,
                dst_ref=ref,
                send_sem=send_sem.at[self.n, k],
                recv_sem=recv_sem.at[self.n, k],
                device_id={"tile": peer},
            )

        def send(self, ref, peer, k):
            copy = self.copy(ref, peer, k)
            copy.start()
            pending.append(copy)

        def block(self, ring, by, half=None):
            ref = self.at(*self.place(ring, by), c)
            if half is None:
                return ref
            return ref.at[pl.ds(half * (self.rows // 2), self.rows // 2)]

        def open(self, ring):
            for k, by in enumerate((1, -1)):
                self.send(self.block(ring, 0), self.peer(ring, by), 4 * ring + k)

        def relay(self, ring):
            for k, by in enumerate((-1, 1)):
                self.copy(self.block(ring, by), self.peer(ring, by), 4 * ring + k).wait_recv()
                self.send(self.block(ring, by, k), self.peer(ring, -by), 4 * ring + 2 + k)
                if ring == 0:
                    self.open(2 + k)

        def close(self, ring):
            for k, by in enumerate((-1, 1)):
                self.copy(self.block(ring, 2, k), self.peer(ring, by), 4 * ring + 2 + k).wait_recv()
            if ring == 0:
                self.open(4)
            else:
                self.send(self.line(ring, c), sibling, 19 + ring)

        def line(self, ring, core):
            return self.at(self.place(ring, 0)[0], slice(None), core)

        def from_sibling(self, ring):
            self.copy(self.line(ring, 1 - c), sibling, 19 + ring).wait_recv()

    def of(buf, which, tile):
        block = blocks_ref[which, tile]
        return buf[block >> 3, (block >> 1) & 3, block & 1]

    def encode(start, stop):
        @pl.loop(start, stop, unroll=4)
        def _(q):
            tile = t * count + q
            half = dot(of(bases, 0, tile), tiles[q], 0, 0).astype(BF16)
            encoded[q] = dot(half, of(bases, 1, tile), 1, 0)

    both = (Gather(0, bases, True), Gather(1, proj, False))
    for step, ring in (
        ("open", 0), ("open", 1), ("relay", 0), ("relay", 1), ("close", 0), ("relay", 2),
        ("relay", 3), ("close", 1), ("relay", 4), ("close", 2), ("close", 3), ("close", 4),
        ("from_sibling", 1), ("from_sibling", 2), ("from_sibling", 3), ("from_sibling", 4),
    ):
        for gather in both:
            getattr(gather, step)(ring)
    keep_bases = pltpu.make_async_copy(bases, bases_out, own_sem.at[1])
    keep_bases.start()
    load_tiles.wait()
    encode(0, count)

    @pl.loop(0, count, unroll=4)
    def _(q):
        tile = t * count + q
        cross = dot(of(proj, 0, tile), of(proj, 1, tile), 1, 1)
        cores[q] = (encoded[q] - cross).astype(BF16)

    dests = [dest_ref[t * count + q] for q in range(count)]

    def partner(step, sign):
        off = lax.rem(step * 11, owners)
        dx, dz, dc = off // 8, lax.rem(off // 2, SIDE), lax.rem(off, 2)
        px, pz, pc = shift(x, sign * dx), shift(z, sign * dz), lax.rem(c + dc, 2)
        return px * 8 + pz * 2 + pc

    def outbound(step, source, target):
        return pltpu.make_async_remote_copy(
            src_ref=outgoing.at[step],
            dst_ref=cores_out.at[source],
            send_sem=a2a_send.at[step],
            recv_sem=a2a_recv.at[step],
            device_id={"tile": target},
        )

    def pack(step, target):
        first, last = jnp.int32(0), jnp.int32(0)
        for q in range(count):
            last = jnp.where(dests[q] == target, q, last)
            back = count - 1 - q
            first = jnp.where(dests[back] == target, back, first)
        outgoing[step, 0] = cores[first]
        outgoing[step, 1] = cores[last]

    @pl.loop(1, owners)
    def _(step):
        target = partner(step, 1)
        pack(step, target)
        outbound(step, t, target).start()

    pack(0, t)
    keep_own = pltpu.make_async_copy(outgoing.at[0], cores_out.at[t], own_sem.at[0])
    keep_own.start()

    @pl.loop(0, owners)
    def _(source):
        first, last, found = jnp.int32(0), jnp.int32(0), jnp.int32(0)
        for q in range(count):
            tile = source * count + q
            hit = dest_ref[tile] == t
            last = jnp.where(hit, tile, last)
            first = jnp.where(hit & (found == 0), tile, first)
            found = found + hit.astype(jnp.int32)
        for k, tile in enumerate((first, last)):
            entry = blocks_ref[0, tile] + blocks_ref[1, tile] * 256 + slot_ref[tile] * 65536
            table_ref[source * CAP + k] = jnp.where(found > k, entry, -1)

    @pl.loop(1, owners)
    def _(step):
        source = partner(step, -1)
        outbound(step, source, source).wait()

    keep_own.wait()
    keep_bases.wait()
    for copy in pending:
        copy.wait_send()


def decode_kernel(
    table_ref,
    pblocks_ref,
    bases_hbm,
    cores_hbm,
    parents_hbm,
    test_hbm,
    updated_hbm,
    sketch,
    bases,
    cores,
    parents,
    test,
    total,
    part,
    number_of,
    listed,
    load_sem,
    tile_sem,
    store_sem,
):
    held = parents.shape[0]
    blocks, places = part.shape[0], cores.shape[0]
    rank = cores.shape[1]

    def load(p):
        return pltpu.make_async_copy(parents_hbm.at[p], parents.at[p], tile_sem.at[p])

    def store(p):
        return pltpu.make_async_copy(parents.at[p], updated_hbm.at[p], store_sem.at[p])

    load_cores = pltpu.make_async_copy(cores_hbm, cores, load_sem.at[0])
    load_bases = pltpu.make_async_copy(bases_hbm, bases, load_sem.at[1])
    load_test = pltpu.make_async_copy(test_hbm, test, load_sem.at[2])
    load_cores.start()
    load_bases.start()
    for p in range(held):
        load(p).start()
    load_test.start()

    @pl.loop(0, blocks)
    def _(b):
        part[b] = jnp.zeros_like(part[b])

    for p in range(held):
        number_of[p] = 0

    @pl.loop(0, places)
    def _(k):
        entry = table_ref[k]

        @pl.when(entry >= 0)
        def _():
            slot = entry >> 16
            n = number_of[slot]
            listed[slot * places + n] = k
            number_of[slot] = n + 1

    empty = jnp.zeros((rank, rank), BF16)
    load_cores.wait()
    load_bases.wait()
    load_test.wait()

    @pl.loop(0, held)
    def _(p):
        load(p).wait()
        total[...] = parents[p].astype(F32)
        n = number_of[p]

        def add(at, wide):
            lefts, rights = [], []
            for pair in range(0, wide, 2):
                rows, cols, middle = [], [], []
                for one in (at + pair, at + pair + 1):
                    k = listed[p * places + jnp.minimum(one, n - 1)]
                    entry = table_ref[k]
                    rows.append(bases[entry & 255])
                    cols.append(bases[(entry >> 8) & 255])
                    middle.append(jnp.where(one < n, cores[k], empty))
                block = jnp.concatenate(
                    [
                        jnp.concatenate([middle[0], empty], axis=1),
                        jnp.concatenate([empty, middle[1]], axis=1),
                    ],
                    axis=0,
                )
                left = dot(jnp.concatenate(rows, axis=1), block, 1, 0)
                lefts.append(left.astype(BF16))
                rights += cols
            left = jnp.concatenate(lefts, axis=1)
            total[...] += dot(left, jnp.concatenate(rights, axis=1), 1, 1)

        fours = (n + 1) // 4

        @pl.loop(0, fours)
        def _(m):
            add(4 * m, 4)

        @pl.when(4 * fours < n)
        def _():
            add(4 * fours, 2)

        new = total[...].astype(BF16)
        parents[p] = new
        store(p).start()
        a, b = pblocks_ref[0, p], pblocks_ref[1, p]
        part[a] += dot(new, test[b], 1, 0)

        @pl.when(a != b)
        def _():
            part[b] += dot(new, test[a], 0, 0)

    @pl.loop(0, blocks)
    def _(b):
        sketch[b] = part[b].astype(BF16)

    for p in range(held):
        store(p).wait()


def reduce_kernel(part, out_ref, *scratch):
    n = len(SPLIT)
    heard, held, got1, held2, got2, held3, got3 = (
        scratch[i * n : (i + 1) * n] for i in range(7)
    )
    send_sem, recv_sem = scratch[7 * n :]
    y, t = lax.axis_index("child"), lax.axis_index("tile")
    x, z, c = t // 8, lax.rem(t // 2, SIDE), lax.rem(t, 2)
    here = (y, x, z)

    def device(coords, core):
        return {"child": coords[0], "tile": coords[1] * 8 + coords[2] * 2 + core}

    def moved(axis, by):
        return tuple(shift(p, by) if a == axis else p for a, p in enumerate(here))

    sibling = device(here, 1 - c)
    greet([sibling] + [device(moved(a, by), c) for a in range(3) for by in (1, 2, 3)])

    await_greetings(10)

    pending = []

    def remote(src, dst, number, peer):
        copy = pltpu.make_async_remote_copy(
            src_ref=src,
            dst_ref=dst,
            send_sem=send_sem.at[number],
            recv_sem=recv_sem.at[number],
            device_id=peer,
        )
        pending.append(copy)
        copy.start()
        return copy

    swaps = [
        remote(part.at[:, :, :, 1 - c, pl.ds(at, rows)], heard[k], 30 + k, sibling)
        for k, (at, rows) in enumerate(SPLIT)
    ]

    def pick(ref, axis, which):
        return ref.at[(slice(None),) * axis + (which,)]

    def left_axes(k, stage):
        axes = [a for a in range(3) if a not in ORDERS[k][:stage]]
        return axes.index(ORDERS[k][stage])

    def scatter(k, stage, buf, got):
        axis, copies = ORDERS[k][stage], []
        at = left_axes(k, stage)
        for by in (1, 3, 2):
            copies.append(
                remote(
                    pick(buf, at, shift(here[axis], by)),
                    got.at[by - 1],
                    9 * k + 3 * stage + by - 1,
                    device(moved(axis, by), c),
                )
            )
        return copies

    def gather_up(k, stage, buf, got, copies, dst):
        axis = ORDERS[k][stage]
        for copy in copies:
            copy.wait_recv()
        kept = pick(buf, left_axes(k, stage), here[axis])[...].astype(F32)
        value = kept + got[0].astype(F32) + got[1].astype(F32) + got[2].astype(F32)
        dst[...] = value.astype(dst.dtype)

    flying = []
    for k, (at, rows) in enumerate(SPLIT):
        swaps[k].wait_recv()

        @pl.loop(0, SIDE)
        def _(a):
            mine = part[a, :, :, c, pl.ds(at, rows)].astype(F32)
            held[k][a] = (mine + heard[k][a].astype(F32)).astype(BF16)

        flying.append(scatter(k, 0, held[k], got1[k]))
    for k in range(n):
        gather_up(k, 0, held[k], got1[k], flying[k], held2[k])
        flying[k] = scatter(k, 1, held2[k], got2[k])
    for k in range(n):
        gather_up(k, 1, held2[k], got2[k], flying[k], held3[k])
        flying[k] = scatter(k, 2, held3[k], got3[k])
    for k, (at, rows) in enumerate(SPLIT):
        gather_up(k, 2, held3[k], got3[k], flying[k], out_ref.at[pl.ds(at, rows)])
    for copy in pending:
        copy.wait_send()


def shards(
    child_tiles,
    panel,
    bases,
    tile_blocks,
    tile_dest,
    tile_slot,
    parent_tiles,
    parent_blocks,
    sketch_test,
):
    owners = lax.axis_size("tile")
    _, count, order, _ = child_tiles.shape
    rank = bases.shape[2]
    width = sketch_test.shape[1]
    held = parent_tiles.shape[1]
    blocks = sketch_test.shape[0] // order
    chunk = sketch_test.shape[0] // (SIDE**3 * 2)
    hbm = pl.BlockSpec(memory_space=pltpu.HBM)
    smem = pl.BlockSpec(memory_space=pltpu.SMEM)
    vmem = pl.BlockSpec(memory_space=pltpu.VMEM)
    dma = pltpu.SemaphoreType.DMA

    whole_bases, cores, table = pl.pallas_call(
        functools.partial(route_kernel, owners),
        out_shape=(
            jax.ShapeDtypeStruct((SIDE, SIDE, 2, order, rank), BF16),
            jax.ShapeDtypeStruct((owners, CAP, rank, rank), BF16),
            jax.ShapeDtypeStruct((owners * CAP,), jnp.int32),
        ),
        in_specs=[smem, smem, smem, hbm, hbm, hbm],
        out_specs=(hbm, hbm, smem),
        scratch_shapes=[
            pltpu.VMEM((count, order, order), BF16),
            pltpu.VMEM((order, order), BF16),
            pltpu.VMEM((SIDE, SIDE, 2, order, rank), BF16),
            pltpu.VMEM((SIDE, SIDE, 2, rank, order), BF16),
            pltpu.VMEM((count, rank, rank), F32),
            pltpu.VMEM((count, rank, rank), BF16),
            pltpu.VMEM((owners, CAP, rank, rank), BF16),
            dma((3,)),
            dma((2,)),
            dma((2, 24)),
            dma((2, 24)),
            dma((owners,)),
            dma((owners,)),
        ],
        compiler_params=pltpu.CompilerParams(
            collective_id=0, has_side_effects=True, vmem_limit_bytes=54 << 20
        ),
        name="encode_and_route",
    )(tile_blocks[0].T, tile_dest[0, :, 0], tile_slot[0], panel[0], bases[0], child_tiles[0])

    updated, part = pl.pallas_call(
        decode_kernel,
        out_shape=(
            jax.ShapeDtypeStruct((held, order, order), BF16),
            jax.ShapeDtypeStruct((blocks, order, width), BF16),
        ),
        in_specs=[smem, smem, hbm, hbm, hbm, hbm],
        out_specs=(hbm, vmem),
        scratch_shapes=[
            pltpu.VMEM((owners, order, rank), BF16),
            pltpu.VMEM((owners * CAP, rank, rank), BF16),
            pltpu.VMEM((held, order, order), BF16),
            pltpu.VMEM((blocks, order, width), BF16),
            pltpu.VMEM((order, order), F32),
            pltpu.VMEM((blocks, order, width), F32),
            pltpu.SMEM((held,), jnp.int32),
            pltpu.SMEM((held * owners * CAP,), jnp.int32),
            dma((3,)),
            dma((held,)),
            dma((held,)),
        ],
        compiler_params=pltpu.CompilerParams(vmem_limit_bytes=34 << 20),
        name="decode_and_sketch",
    )(
        table,
        parent_blocks[0].T,
        whole_bases.reshape(owners, order, rank),
        cores.reshape(owners * CAP, rank, rank),
        parent_tiles[0],
        sketch_test.reshape(blocks, order, width),
    )

    def bufs(*lead):
        return [pltpu.VMEM((*lead, rows, width), BF16) for _, rows in SPLIT]

    row_sketch = pl.pallas_call(
        reduce_kernel,
        out_shape=jax.ShapeDtypeStruct((chunk, width), F32),
        in_specs=[vmem],
        out_specs=vmem,
        scratch_shapes=[
            *bufs(4, 4, 4),
            *bufs(4, 4, 4),
            *bufs(3, 4, 4),
            *bufs(4, 4),
            *bufs(3, 4),
            *bufs(4),
            *bufs(3),
            dma((33,)),
            dma((33,)),
        ],
        compiler_params=pltpu.CompilerParams(
            collective_id=1, has_side_effects=True, vmem_limit_bytes=32 << 20
        ),
        name="reduce_sketch",
    )(part.reshape(SIDE, SIDE, SIDE, 2, chunk, width))
    return (updated[None], row_sketch)


def solution(mesh):
    return jax.shard_map(
        shards,
        mesh=mesh,
        in_specs=(
            P("child", "tile", None, None),
            P("child", "tile", None),
            P("child", "tile", None),
            P("child", None, None),
            P("child", None, None),
            P("child", None),
            P("child", "tile", None, None),
            P("child", "tile", None),
            P(),
        ),
        out_specs=(P("child", "tile", None, None), P(("child", "tile"), None)),
        check_vma=False,
    )
```

```python
import functools

import jax
import jax.numpy as jnp
from jax import lax
from jax.experimental import pallas as pl
from jax.experimental.pallas import tpu as pltpu
from jax.sharding import PartitionSpec as P

CAP = 2
SIDE = 4
F32 = jnp.float32
BF16 = jnp.bfloat16
PLAN = (
    (0, 0), (0, 1), (5, 0), (0, 2), (0, 3), (0, 4), (0, 5), (0, 6), (1, 0), (1, 1), (0, 7), (0, 8),
    (0, 9), (0, 10), (0, 11), (1, 2), (1, 3), (0, 12), (0, 13), (0, 14), (0, 15), (1, 4),
    (2, 0), (1, 5), (2, 1), (1, 6), (2, 2), (1, 7), (2, 3), (1, 8),
    (3, 0), (1, 9), (3, 1), (1, 10), (3, 2), (1, 11), (3, 3), (4, 0), (1, 12), (1, 13), (1, 14), (1, 15),
)
SHARED = 40
SPLIT = ((0, 48), (48, 48), (96, 32))
ORDERS = ((0, 1, 2), (1, 2, 0), (2, 0, 1))


def dot(a, b, ca, cb):
    return lax.dot_general(a, b, (((ca,), (cb,)), ((), ())), preferred_element_type=F32)


def shift(p, by):
    return lax.rem(p + by + SIDE, SIDE)


def greet(devices):
    barrier = pltpu.get_barrier_semaphore()
    for device in devices:
        pl.semaphore_signal(barrier, inc=1, device_id=device)


def await_greetings(count):
    pl.semaphore_wait(pltpu.get_barrier_semaphore(), count)


def route_kernel(
    owners,
    blocks_ref,
    dest_ref,
    slot_ref,
    panel_hbm,
    bases_hbm,
    tiles_hbm,
    shared,
    table_ref,
    tiles,
    panel,
    bases,
    proj,
    cores,
    outgoing,
    incoming,
    settled,
    load_sem,
    own_sem,
    keep_sem,
    send_sem,
    recv_sem,
    a2a_send,
    a2a_recv,
):
    t = lax.axis_index("tile")
    x, z, c = t // 8, lax.rem(t // 2, SIDE), lax.rem(t, 2)
    count, rank = tiles.shape[0], cores.shape[1]

    load_panel = pltpu.make_async_copy(panel_hbm, panel, load_sem.at[0])
    load_bases = pltpu.make_async_copy(bases_hbm, bases.at[x, z, c], load_sem.at[1])
    load_tiles = pltpu.make_async_copy(tiles_hbm, tiles, load_sem.at[2])
    load_bases.start()
    load_panel.start()
    load_tiles.start()

    @pl.loop(1, owners)
    def _(step):
        pl.semaphore_signal(
            pltpu.get_barrier_semaphore(),
            inc=1,
            device_id={"tile": lax.rem(t + step, owners)},
        )

    load_bases.wait()
    await_greetings(owners - 1)

    sibling = t + 1 - 2 * c
    pending = []

    class Gather:
        offsets = (None, 0, -1, 1, 2)

        def __init__(self, number, buf, x_first):
            self.n, self.buf, self.x_first = number, buf, x_first
            self.f, self.s = (x, z) if x_first else (z, x)
            self.rows = buf.shape[3] // 2
            self.start = 0 if x_first else self.rows

        def at(self, first, second, core, at=0, rows=None):
            place = (first, second) if self.x_first else (second, first)
            return self.buf.at[(*place, core, pl.ds(self.start + at, rows or self.rows))]

        def place(self, ring, by):
            if ring == 0:
                return shift(self.f, by), self.s
            return shift(self.f, self.offsets[ring]), shift(self.s, by)

        def peer(self, ring, by):
            first, second = (self.f, shift(self.s, by)) if ring else self.place(0, by)
            return (first if self.x_first else second) * 8 + (second if self.x_first else first) * 2 + c

        def copy(self, ref, peer, k):
            return pltpu.make_async_remote_copy(
                src_ref=ref,
                dst_ref=ref,
                send_sem=send_sem.at[self.n, k],
                recv_sem=recv_sem.at[self.n, k],
                device_id={"tile": peer},
            )

        def send(self, ref, peer, k):
            copy = self.copy(ref, peer, k)
            copy.start()
            pending.append(copy)

        def block(self, ring, by, half=None):
            if half is None:
                return self.at(*self.place(ring, by), c)
            return self.at(*self.place(ring, by), c, half * (self.rows // 2), self.rows // 2)

        def open(self, ring):
            for k, by in enumerate((1, -1) if ring else (1, -1, 2)):
                self.send(self.block(ring, 0), self.peer(ring, by), 4 * ring + k)

        def relay(self, ring):
            for k, by in enumerate((-1, 1)):
                self.copy(self.block(ring, by), self.peer(ring, by), 4 * ring + k).wait_recv()
                if ring:
                    self.send(self.block(ring, by, k), self.peer(ring, -by), 4 * ring + 2 + k)
                else:
                    self.open(2 + k)

        def close(self, ring):
            if ring == 0:
                self.copy(self.block(0, 2), self.peer(0, 2), 2).wait_recv()
                self.open(4)
                return
            for k, by in enumerate((-1, 1)):
                self.copy(self.block(ring, 2, k), self.peer(ring, by), 4 * ring + 2 + k).wait_recv()
            self.send(self.line(ring, c), sibling, 19 + ring)

        def line(self, ring, core):
            return self.at(self.place(ring, 0)[0], slice(None), core)

        def from_sibling(self, ring):
            self.copy(self.line(ring, 1 - c), sibling, 19 + ring).wait_recv()

    def of(buf, which, tile):
        block = blocks_ref[which, tile]
        return buf[block >> 3, (block >> 1) & 3, block & 1]

    def encode(start, stop):
        @pl.loop(start, stop, unroll=4)
        def _(q):
            tile = t * count + q
            half = dot(of(bases, 0, tile), tiles[q], 0, 0).astype(BF16)
            cores[q] = dot(half, of(bases, 1, tile), 1, 0).astype(BF16)

    steps = (
        ("open", 0), ("open", 1), ("relay", 0), ("relay", 1), ("close", 0), ("relay", 2),
        ("relay", 3), ("close", 1), ("relay", 4), ("close", 2), ("close", 3), ("close", 4),
        ("from_sibling", 1), ("from_sibling", 2), ("from_sibling", 3), ("from_sibling", 4),
    )
    arrays = (
        (Gather(0, bases, True), Gather(1, bases, False)),
        (Gather(2, proj, True), Gather(3, proj, False)),
    )
    dests = [dest_ref[t * count + q] for q in range(count)]

    def partner(step, sign):
        off = lax.rem(step * 11, owners)
        dx, dz, dc = off // 8, lax.rem(off // 2, SIDE), lax.rem(off, 2)
        px, pz, pc = shift(x, sign * dx), shift(z, sign * dz), lax.rem(c + dc, 2)
        return px * 8 + pz * 2 + pc

    def outbound(step, source, target):
        return pltpu.make_async_remote_copy(
            src_ref=outgoing.at[step],
            dst_ref=incoming.at[source],
            send_sem=a2a_send.at[step],
            recv_sem=a2a_recv.at[step],
            device_id={"tile": target},
        )

    def pack(step, target):
        first, last = jnp.int32(0), jnp.int32(0)
        for q in range(count):
            last = jnp.where(dests[q] == target, q, last)
            back = count - 1 - q
            first = jnp.where(dests[back] == target, back, first)
        outgoing[step, 0] = cores[first]
        outgoing[step, 1] = cores[last]

    def dispatch(start, stop):
        @pl.loop(max(start, 1), stop)
        def _(step):
            target = partner(step, 1)
            pack(step, target)
            outbound(step, t, target).start()

    def foretell():
        @pl.loop(0, owners)
        def _(source):
            first, last, found = jnp.int32(0), jnp.int32(0), jnp.int32(0)
            for q in range(count):
                tile = source * count + q
                hit = dest_ref[tile] == t
                last = jnp.where(hit, tile, last)
                first = jnp.where(hit & (found == 0), tile, first)
                found = found + hit.astype(jnp.int32)
            for k, tile in enumerate((first, last)):
                entry = blocks_ref[0, tile] + blocks_ref[1, tile] * 256 + slot_ref[tile] * 65536
                table_ref[source * CAP + k] = jnp.where(found > k, entry, -1)

    each, wave = count // 4, owners // 4
    for what, at in PLAN:
        if what == 2:
            if at == 0:
                keep_bases = pltpu.make_async_copy(bases, shared.at[pl.ds(0, SIDE)], own_sem.at[1])
                keep_bases.start()
                load_tiles.wait()
            encode(at * each, at * each + each)
        elif what == 3:
            dispatch(at * wave, at * wave + wave)
        elif what == 4:
            foretell()
        elif what == 5:
            load_panel.wait()
            proj[x, z, c] = dot(bases[x, z, c], panel[...], 0, 0).astype(BF16)
        else:
            step, ring = steps[at]
            for gather in arrays[what]:
                getattr(gather, step)(ring)

    def keep(source):
        place = (source // 16, lax.rem(source // 4, SIDE), lax.rem(source // 2, 2))
        rows = pl.ds(pl.multiple_of(lax.rem(source, 2) * CAP * rank, CAP * rank), CAP * rank)
        return pltpu.make_async_copy(
            settled.at[source],
            shared.at[SIDE + place[0], place[1], place[2], rows],
            keep_sem.at[source],
        )

    def settle(source, received):
        for k in range(CAP):
            entry = jnp.maximum(table_ref[source * CAP + k], 0)
            i, j = entry & 255, (entry >> 8) & 255
            cross = dot(
                proj[i >> 3, (i >> 1) & 3, i & 1], proj[j >> 3, (j >> 1) & 3, j & 1], 1, 1
            )
            core = received[k].astype(F32) - cross
            settled[source, k * rank : (k + 1) * rank] = core.astype(BF16)
        keep(source).start()

    pack(0, t)
    settle(t, outgoing.at[0])

    @pl.loop(1, owners)
    def _(step):
        source = partner(step, -1)
        outbound(step, source, source).wait()
        settle(source, incoming.at[source])

    @pl.loop(0, owners)
    def _(source):
        keep(source).wait()

    keep_bases.wait()
    for copy in pending:
        copy.wait_send()


def decode_kernel(
    table_ref,
    pblocks_ref,
    shared,
    parents_hbm,
    test_hbm,
    updated_hbm,
    sketch,
    bases,
    cores,
    parents,
    test,
    total,
    part,
    number_of,
    listed,
    load_sem,
    tile_sem,
    store_sem,
):
    held = parents.shape[0]
    blocks, places = part.shape[0], table_ref.shape[0]
    rank = cores.shape[4]

    def load(p):
        return pltpu.make_async_copy(parents_hbm.at[p], parents.at[p], tile_sem.at[p])

    def store(p):
        return pltpu.make_async_copy(parents.at[p], updated_hbm.at[p], store_sem.at[p])

    load_cores = pltpu.make_async_copy(shared.at[pl.ds(SIDE, 2)], cores, load_sem.at[0])
    load_bases = pltpu.make_async_copy(shared.at[pl.ds(0, SIDE)], bases, load_sem.at[1])
    load_test = pltpu.make_async_copy(test_hbm, test, load_sem.at[2])
    load_cores.start()
    load_bases.start()
    for p in range(held):
        load(p).start()
    load_test.start()

    @pl.loop(0, blocks)
    def _(b):
        part[b] = jnp.zeros_like(part[b])

    for p in range(held):
        number_of[p] = 0

    @pl.loop(0, places)
    def _(k):
        entry = table_ref[k]

        @pl.when(entry >= 0)
        def _():
            slot = entry >> 16
            n = number_of[slot]
            listed[slot * places + n] = k
            number_of[slot] = n + 1

    def basis(block):
        return bases[block >> 3, (block >> 1) & 3, block & 1]

    def core(k):
        rows = pl.ds(pl.multiple_of((k & 3) * rank, rank), rank)
        return cores[k >> 5, (k >> 3) & 3, (k >> 2) & 1, rows]

    empty = jnp.zeros((rank, rank), BF16)
    load_cores.wait()
    load_bases.wait()
    load_test.wait()

    @pl.loop(0, held)
    def _(p):
        load(p).wait()
        total[...] = parents[p].astype(F32)
        n = number_of[p]

        def add(at, wide):
            lefts, rights = [], []
            for pair in range(0, wide, 2):
                rows, cols, middle = [], [], []
                for one in (at + pair, at + pair + 1):
                    k = listed[p * places + jnp.minimum(one, n - 1)]
                    entry = table_ref[k]
                    rows.append(basis(entry & 255))
                    cols.append(basis((entry >> 8) & 255))
                    middle.append(jnp.where(one < n, core(k), empty))
                block = jnp.concatenate(
                    [
                        jnp.concatenate([middle[0], empty], axis=1),
                        jnp.concatenate([empty, middle[1]], axis=1),
                    ],
                    axis=0,
                )
                left = dot(jnp.concatenate(rows, axis=1), block, 1, 0)
                lefts.append(left.astype(BF16))
                rights += cols
            left = jnp.concatenate(lefts, axis=1)
            total[...] += dot(left, jnp.concatenate(rights, axis=1), 1, 1)

        fours = (n + 1) // 4

        @pl.loop(0, fours)
        def _(m):
            add(4 * m, 4)

        @pl.when(4 * fours < n)
        def _():
            add(4 * fours, 2)

        new = total[...].astype(BF16)
        parents[p] = new
        store(p).start()
        a, b = pblocks_ref[0, p], pblocks_ref[1, p]
        part[a] += dot(new, test[b], 1, 0)

        @pl.when(a != b)
        def _():
            part[b] += dot(new, test[a], 0, 0)

    @pl.loop(0, blocks)
    def _(b):
        sketch[b] = part[b].astype(BF16)

    for p in range(held):
        store(p).wait()


def reduce_kernel(part, out_ref, *scratch):
    n = len(SPLIT)
    heard, held, got1, held2, got2, held3, got3 = (
        scratch[i * n : (i + 1) * n] for i in range(7)
    )
    send_sem, recv_sem = scratch[7 * n :]
    y, t = lax.axis_index("child"), lax.axis_index("tile")
    x, z, c = t // 8, lax.rem(t // 2, SIDE), lax.rem(t, 2)
    here = (y, x, z)

    def device(coords, core):
        return {"child": coords[0], "tile": coords[1] * 8 + coords[2] * 2 + core}

    def moved(axis, by):
        return tuple(shift(p, by) if a == axis else p for a, p in enumerate(here))

    sibling = device(here, 1 - c)
    greet([sibling] + [device(moved(a, by), c) for a in range(3) for by in (1, 2, 3)])

    await_greetings(10)

    pending = []

    def remote(src, dst, number, peer):
        copy = pltpu.make_async_remote_copy(
            src_ref=src,
            dst_ref=dst,
            send_sem=send_sem.at[number],
            recv_sem=recv_sem.at[number],
            device_id=peer,
        )
        pending.append(copy)
        copy.start()
        return copy

    swaps = [
        remote(part.at[:, :, :, 1 - c, pl.ds(at, rows)], heard[k], 30 + k, sibling)
        for k, (at, rows) in enumerate(SPLIT)
    ]

    def pick(ref, axis, which):
        return ref.at[(slice(None),) * axis + (which,)]

    def left_axes(k, stage):
        axes = [a for a in range(3) if a not in ORDERS[k][:stage]]
        return axes.index(ORDERS[k][stage])

    def scatter(k, stage, buf, got):
        axis, copies = ORDERS[k][stage], []
        at = left_axes(k, stage)
        for by in (1, 3, 2):
            copies.append(
                remote(
                    pick(buf, at, shift(here[axis], by)),
                    got.at[by - 1],
                    9 * k + 3 * stage + by - 1,
                    device(moved(axis, by), c),
                )
            )
        return copies

    def gather_up(k, stage, buf, got, copies, dst):
        axis = ORDERS[k][stage]
        for copy in copies:
            copy.wait_recv()
        kept = pick(buf, left_axes(k, stage), here[axis])[...].astype(F32)
        value = kept + got[0].astype(F32) + got[1].astype(F32) + got[2].astype(F32)
        dst[...] = value.astype(dst.dtype)

    flying = []
    for k, (at, rows) in enumerate(SPLIT):
        swaps[k].wait_recv()

        @pl.loop(0, SIDE)
        def _(a):
            mine = part[a, :, :, c, pl.ds(at, rows)].astype(F32)
            held[k][a] = (mine + heard[k][a].astype(F32)).astype(BF16)

        flying.append(scatter(k, 0, held[k], got1[k]))
    for k in range(n):
        gather_up(k, 0, held[k], got1[k], flying[k], held2[k])
        flying[k] = scatter(k, 1, held2[k], got2[k])
    for k in range(n):
        gather_up(k, 1, held2[k], got2[k], flying[k], held3[k])
        flying[k] = scatter(k, 2, held3[k], got3[k])
    for k, (at, rows) in enumerate(SPLIT):
        gather_up(k, 2, held3[k], got3[k], flying[k], out_ref.at[pl.ds(at, rows)])
    for copy in pending:
        copy.wait_send()


def shards(
    child_tiles,
    panel,
    bases,
    tile_blocks,
    tile_dest,
    tile_slot,
    parent_tiles,
    parent_blocks,
    sketch_test,
):
    owners = lax.axis_size("tile")
    _, count, order, _ = child_tiles.shape
    rank = bases.shape[2]
    width = sketch_test.shape[1]
    held = parent_tiles.shape[1]
    blocks = sketch_test.shape[0] // order
    chunk = sketch_test.shape[0] // (SIDE**3 * 2)
    hbm = pl.BlockSpec(memory_space=pltpu.HBM)
    smem = pl.BlockSpec(memory_space=pltpu.SMEM)
    vmem = pl.BlockSpec(memory_space=pltpu.VMEM)
    dma = pltpu.SemaphoreType.DMA

    shared, table = pl.pallas_call(
        functools.partial(route_kernel, owners),
        out_shape=(
            jax.ShapeDtypeStruct((SHARED, SIDE, 2, order, rank), BF16),
            jax.ShapeDtypeStruct((owners * CAP,), jnp.int32),
        ),
        in_specs=[smem, smem, smem, hbm, hbm, hbm],
        out_specs=(hbm, smem),
        scratch_shapes=[
            pltpu.VMEM((count, order, order), BF16),
            pltpu.VMEM((order, order), BF16),
            pltpu.VMEM((SIDE, SIDE, 2, order, rank), BF16),
            pltpu.VMEM((SIDE, SIDE, 2, rank, order), BF16),
            pltpu.VMEM((count, rank, rank), BF16),
            pltpu.VMEM((owners, CAP, rank, rank), BF16),
            pltpu.VMEM((owners, CAP, rank, rank), BF16),
            pltpu.VMEM((owners, CAP * rank, rank), BF16),
            dma((3,)),
            dma((2,)),
            dma((owners,)),
            dma((4, 24)),
            dma((4, 24)),
            dma((owners,)),
            dma((owners,)),
        ],
        compiler_params=pltpu.CompilerParams(
            collective_id=0, has_side_effects=True, vmem_limit_bytes=54 << 20
        ),
        name="encode_and_route",
    )(tile_blocks[0].T, tile_dest[0, :, 0], tile_slot[0], panel[0], bases[0], child_tiles[0])

    updated, part = pl.pallas_call(
        decode_kernel,
        out_shape=(
            jax.ShapeDtypeStruct((held, order, order), BF16),
            jax.ShapeDtypeStruct((blocks, order, width), BF16),
        ),
        in_specs=[smem, smem, hbm, hbm, hbm],
        out_specs=(hbm, vmem),
        scratch_shapes=[
            pltpu.VMEM((SIDE, SIDE, 2, order, rank), BF16),
            pltpu.VMEM((2, SIDE, 2, order, rank), BF16),
            pltpu.VMEM((held, order, order), BF16),
            pltpu.VMEM((blocks, order, width), BF16),
            pltpu.VMEM((order, order), F32),
            pltpu.VMEM((blocks, order, width), F32),
            pltpu.SMEM((held,), jnp.int32),
            pltpu.SMEM((held * owners * CAP,), jnp.int32),
            dma((3,)),
            dma((held,)),
            dma((held,)),
        ],
        compiler_params=pltpu.CompilerParams(vmem_limit_bytes=34 << 20),
        name="decode_and_sketch",
    )(
        table,
        parent_blocks[0].T,
        shared,
        parent_tiles[0],
        sketch_test.reshape(blocks, order, width),
    )

    def bufs(*lead):
        return [pltpu.VMEM((*lead, rows, width), BF16) for _, rows in SPLIT]

    row_sketch = pl.pallas_call(
        reduce_kernel,
        out_shape=jax.ShapeDtypeStruct((chunk, width), F32),
        in_specs=[vmem],
        out_specs=vmem,
        scratch_shapes=[
            *bufs(4, 4, 4),
            *bufs(4, 4, 4),
            *bufs(3, 4, 4),
            *bufs(4, 4),
            *bufs(3, 4),
            *bufs(4),
            *bufs(3),
            dma((33,)),
            dma((33,)),
        ],
        compiler_params=pltpu.CompilerParams(
            collective_id=1, has_side_effects=True, vmem_limit_bytes=32 << 20
        ),
        name="reduce_sketch",
    )(part.reshape(SIDE, SIDE, SIDE, 2, chunk, width))
    return (updated[None], row_sketch)


def solution(mesh):
    return jax.shard_map(
        shards,
        mesh=mesh,
        in_specs=(
            P("child", "tile", None, None),
            P("child", "tile", None),
            P("child", "tile", None),
            P("child", None, None),
            P("child", None, None),
            P("child", None),
            P("child", "tile", None, None),
            P("child", "tile", None),
            P(),
        ),
        out_specs=(P("child", "tile", None, None), P(("child", "tile"), None)),
        check_vma=False,
    )
```

```python
import functools

import jax
import jax.numpy as jnp
from jax import lax
from jax.experimental import pallas as pl
from jax.experimental.pallas import tpu as pltpu
from jax.sharding import PartitionSpec as P

CAP = 2
SIDE = 4
F32 = jnp.float32
BF16 = jnp.bfloat16
PLAN = (
    (0, 0), (0, 1), (5, 0), (0, 2), (0, 3), (0, 4), (0, 5), (0, 6), (1, 0), (1, 1), (0, 7), (0, 8),
    (0, 9), (0, 10), (0, 11), (1, 2), (1, 3), (0, 12), (0, 13), (0, 14), (0, 15), (1, 4),
    (2, 0), (1, 5), (2, 1), (1, 6), (2, 2), (1, 7), (2, 3), (1, 8),
    (3, 0), (1, 9), (3, 1), (1, 10), (3, 2), (1, 11), (3, 3), (4, 0), (1, 12), (1, 13), (1, 14), (1, 15),
)
SHARED = 40
SPLIT = ((0, 32), (32, 32), (64, 16), (80, 16), (96, 16), (112, 16))
ORDERS = ((0, 1, 2), (1, 2, 0), (2, 0, 1)) * 2


def dot(a, b, ca, cb):
    return lax.dot_general(a, b, (((ca,), (cb,)), ((), ())), preferred_element_type=F32)


def shift(p, by):
    return lax.rem(p + by + SIDE, SIDE)


def greet(devices):
    barrier = pltpu.get_barrier_semaphore()
    for device in devices:
        pl.semaphore_signal(barrier, inc=1, device_id=device)


def await_greetings(count):
    pl.semaphore_wait(pltpu.get_barrier_semaphore(), count)


def route_kernel(
    owners,
    blocks_ref,
    dest_ref,
    slot_ref,
    panel_hbm,
    bases_hbm,
    tiles_hbm,
    shared,
    table_ref,
    tiles,
    panel,
    bases,
    proj,
    cores,
    outgoing,
    incoming,
    settled,
    load_sem,
    own_sem,
    keep_sem,
    send_sem,
    recv_sem,
    a2a_send,
    a2a_recv,
):
    t = lax.axis_index("tile")
    x, z, c = t // 8, lax.rem(t // 2, SIDE), lax.rem(t, 2)
    count, rank = tiles.shape[0], cores.shape[1]

    load_panel = pltpu.make_async_copy(panel_hbm, panel, load_sem.at[0])
    load_bases = pltpu.make_async_copy(bases_hbm, bases.at[x, z, c], load_sem.at[1])
    load_tiles = pltpu.make_async_copy(tiles_hbm, tiles, load_sem.at[2])
    load_bases.start()
    load_panel.start()
    load_tiles.start()

    @pl.loop(1, owners)
    def _(step):
        pl.semaphore_signal(
            pltpu.get_barrier_semaphore(),
            inc=1,
            device_id={"tile": lax.rem(t + step, owners)},
        )

    load_bases.wait()
    await_greetings(owners - 1)

    sibling = t + 1 - 2 * c
    pending = []

    class Gather:
        offsets = (None, 0, -1, 1, 2)

        def __init__(self, number, buf, x_first):
            self.n, self.buf, self.x_first = number, buf, x_first
            self.f, self.s = (x, z) if x_first else (z, x)
            self.rows = buf.shape[3] // 2
            self.start = 0 if x_first else self.rows

        def at(self, first, second, core, at=0, rows=None):
            place = (first, second) if self.x_first else (second, first)
            return self.buf.at[(*place, core, pl.ds(self.start + at, rows or self.rows))]

        def place(self, ring, by):
            if ring == 0:
                return shift(self.f, by), self.s
            return shift(self.f, self.offsets[ring]), shift(self.s, by)

        def peer(self, ring, by):
            first, second = (self.f, shift(self.s, by)) if ring else self.place(0, by)
            return (first if self.x_first else second) * 8 + (second if self.x_first else first) * 2 + c

        def copy(self, ref, peer, k):
            return pltpu.make_async_remote_copy(
                src_ref=ref,
                dst_ref=ref,
                send_sem=send_sem.at[self.n, k],
                recv_sem=recv_sem.at[self.n, k],
                device_id={"tile": peer},
            )

        def send(self, ref, peer, k):
            copy = self.copy(ref, peer, k)
            copy.start()
            pending.append(copy)

        def block(self, ring, by, half=None):
            if half is None:
                return self.at(*self.place(ring, by), c)
            return self.at(*self.place(ring, by), c, half * (self.rows // 2), self.rows // 2)

        def open(self, ring):
            for k, by in enumerate((1, -1) if ring else (1, -1, 2)):
                self.send(self.block(ring, 0), self.peer(ring, by), 4 * ring + k)

        def relay(self, ring):
            for k, by in enumerate((-1, 1)):
                self.copy(self.block(ring, by), self.peer(ring, by), 4 * ring + k).wait_recv()
                if ring:
                    self.send(self.block(ring, by, k), self.peer(ring, -by), 4 * ring + 2 + k)
                else:
                    self.open(2 + k)

        def close(self, ring):
            if ring == 0:
                self.copy(self.block(0, 2), self.peer(0, 2), 2).wait_recv()
                self.open(4)
                return
            for k, by in enumerate((-1, 1)):
                self.copy(self.block(ring, 2, k), self.peer(ring, by), 4 * ring + 2 + k).wait_recv()
            self.send(self.line(ring, c), sibling, 19 + ring)

        def line(self, ring, core):
            return self.at(self.place(ring, 0)[0], slice(None), core)

        def from_sibling(self, ring):
            self.copy(self.line(ring, 1 - c), sibling, 19 + ring).wait_recv()

    def of(buf, which, tile):
        block = blocks_ref[which, tile]
        return buf[block >> 3, (block >> 1) & 3, block & 1]

    def encode(start, stop):
        @pl.loop(start, stop, unroll=4)
        def _(q):
            tile = t * count + q
            half = dot(of(bases, 0, tile), tiles[q], 0, 0).astype(BF16)
            cores[q] = dot(half, of(bases, 1, tile), 1, 0).astype(BF16)

    steps = (
        ("open", 0), ("open", 1), ("relay", 0), ("relay", 1), ("close", 0), ("relay", 2),
        ("relay", 3), ("close", 1), ("relay", 4), ("close", 2), ("close", 3), ("close", 4),
        ("from_sibling", 1), ("from_sibling", 2), ("from_sibling", 3), ("from_sibling", 4),
    )
    arrays = (
        (Gather(0, bases, True), Gather(1, bases, False)),
        (Gather(2, proj, True), Gather(3, proj, False)),
    )
    dests = [dest_ref[t * count + q] for q in range(count)]

    def partner(step, sign):
        off = lax.rem(step * 11, owners)
        dx, dz, dc = off // 8, lax.rem(off // 2, SIDE), lax.rem(off, 2)
        px, pz, pc = shift(x, sign * dx), shift(z, sign * dz), lax.rem(c + dc, 2)
        return px * 8 + pz * 2 + pc

    def outbound(step, source, target):
        return pltpu.make_async_remote_copy(
            src_ref=outgoing.at[step],
            dst_ref=incoming.at[source],
            send_sem=a2a_send.at[step],
            recv_sem=a2a_recv.at[step],
            device_id={"tile": target},
        )

    def pack(step, target):
        first, last = jnp.int32(0), jnp.int32(0)
        for q in range(count):
            last = jnp.where(dests[q] == target, q, last)
            back = count - 1 - q
            first = jnp.where(dests[back] == target, back, first)
        outgoing[step, 0] = cores[first]
        outgoing[step, 1] = cores[last]

    def dispatch(start, stop):
        @pl.loop(max(start, 1), stop)
        def _(step):
            target = partner(step, 1)
            pack(step, target)
            outbound(step, t, target).start()

    def foretell():
        @pl.loop(0, owners)
        def _(source):
            first, last, found = jnp.int32(0), jnp.int32(0), jnp.int32(0)
            for q in range(count):
                tile = source * count + q
                hit = dest_ref[tile] == t
                last = jnp.where(hit, tile, last)
                first = jnp.where(hit & (found == 0), tile, first)
                found = found + hit.astype(jnp.int32)
            for k, tile in enumerate((first, last)):
                entry = blocks_ref[0, tile] + blocks_ref[1, tile] * 256 + slot_ref[tile] * 65536
                table_ref[source * CAP + k] = jnp.where(found > k, entry, -1)

    each, wave = count // 4, owners // 4
    for what, at in PLAN:
        if what == 2:
            if at == 0:
                keep_bases = pltpu.make_async_copy(bases, shared.at[pl.ds(0, SIDE)], own_sem.at[1])
                keep_bases.start()
                load_tiles.wait()
            encode(at * each, at * each + each)
        elif what == 3:
            dispatch(at * wave, at * wave + wave)
        elif what == 4:
            foretell()
        elif what == 5:
            load_panel.wait()
            proj[x, z, c] = dot(bases[x, z, c], panel[...], 0, 0).astype(BF16)
        else:
            step, ring = steps[at]
            for gather in arrays[what]:
                getattr(gather, step)(ring)

    def keep(source):
        place = (source // 16, lax.rem(source // 4, SIDE), lax.rem(source // 2, 2))
        rows = pl.ds(pl.multiple_of(lax.rem(source, 2) * CAP * rank, CAP * rank), CAP * rank)
        return pltpu.make_async_copy(
            settled.at[source],
            shared.at[SIDE + place[0], place[1], place[2], rows],
            keep_sem.at[source],
        )

    def settle(source, received):
        for k in range(CAP):
            entry = jnp.maximum(table_ref[source * CAP + k], 0)
            i, j = entry & 255, (entry >> 8) & 255
            cross = dot(
                proj[i >> 3, (i >> 1) & 3, i & 1], proj[j >> 3, (j >> 1) & 3, j & 1], 1, 1
            )
            core = received[k].astype(F32) - cross
            settled[source, k * rank : (k + 1) * rank] = core.astype(BF16)
        keep(source).start()

    pack(0, t)
    settle(t, outgoing.at[0])

    @pl.loop(1, owners)
    def _(step):
        source = partner(step, -1)
        outbound(step, source, source).wait()
        settle(source, incoming.at[source])

    @pl.loop(0, owners)
    def _(source):
        keep(source).wait()

    keep_bases.wait()
    for copy in pending:
        copy.wait_send()


def decode_kernel(
    table_ref,
    pblocks_ref,
    shared,
    parents_hbm,
    test_hbm,
    updated_hbm,
    sketch,
    bases,
    cores,
    parents,
    test,
    total,
    part,
    number_of,
    listed,
    load_sem,
    tile_sem,
    store_sem,
):
    held = parents.shape[0]
    blocks, places = part.shape[0], table_ref.shape[0]
    rank = cores.shape[4]

    def load(p):
        return pltpu.make_async_copy(parents_hbm.at[p], parents.at[p], tile_sem.at[p])

    def store(p):
        return pltpu.make_async_copy(parents.at[p], updated_hbm.at[p], store_sem.at[p])

    load_cores = pltpu.make_async_copy(shared.at[pl.ds(SIDE, 2)], cores, load_sem.at[0])
    load_bases = pltpu.make_async_copy(shared.at[pl.ds(0, SIDE)], bases, load_sem.at[1])
    load_test = pltpu.make_async_copy(test_hbm, test, load_sem.at[2])
    load_cores.start()
    load_bases.start()
    for p in range(held):
        load(p).start()
    load_test.start()

    @pl.loop(0, blocks)
    def _(b):
        part[b] = jnp.zeros_like(part[b])

    for p in range(held):
        number_of[p] = 0

    @pl.loop(0, places)
    def _(k):
        entry = table_ref[k]

        @pl.when(entry >= 0)
        def _():
            slot = entry >> 16
            n = number_of[slot]
            listed[slot * places + n] = k
            number_of[slot] = n + 1

    def basis(block):
        return bases[block >> 3, (block >> 1) & 3, block & 1]

    def core(k):
        rows = pl.ds(pl.multiple_of((k & 3) * rank, rank), rank)
        return cores[k >> 5, (k >> 3) & 3, (k >> 2) & 1, rows]

    empty = jnp.zeros((rank, rank), BF16)
    load_cores.wait()
    load_bases.wait()
    load_test.wait()

    @pl.loop(0, held)
    def _(p):
        load(p).wait()
        total[...] = parents[p].astype(F32)
        n = number_of[p]

        def add(at, wide):
            lefts, rights = [], []
            for pair in range(0, wide, 2):
                rows, cols, middle = [], [], []
                for one in (at + pair, at + pair + 1):
                    k = listed[p * places + jnp.minimum(one, n - 1)]
                    entry = table_ref[k]
                    rows.append(basis(entry & 255))
                    cols.append(basis((entry >> 8) & 255))
                    middle.append(jnp.where(one < n, core(k), empty))
                block = jnp.concatenate(
                    [
                        jnp.concatenate([middle[0], empty], axis=1),
                        jnp.concatenate([empty, middle[1]], axis=1),
                    ],
                    axis=0,
                )
                left = dot(jnp.concatenate(rows, axis=1), block, 1, 0)
                lefts.append(left.astype(BF16))
                rights += cols
            left = jnp.concatenate(lefts, axis=1)
            total[...] += dot(left, jnp.concatenate(rights, axis=1), 1, 1)

        eights = n // 8

        @pl.loop(0, eights)
        def _(m):
            add(8 * m, 8)

        rest = n - 8 * eights
        fours = (rest + 1) // 4

        @pl.loop(0, fours)
        def _(m):
            add(8 * eights + 4 * m, 4)

        @pl.when(4 * fours < rest)
        def _():
            add(8 * eights + 4 * fours, 2)

        new = total[...].astype(BF16)
        parents[p] = new
        store(p).start()
        a, b = pblocks_ref[0, p], pblocks_ref[1, p]
        part[a] += dot(new, test[b], 1, 0)

        @pl.when(a != b)
        def _():
            part[b] += dot(new, test[a], 0, 0)

    @pl.loop(0, blocks)
    def _(b):
        sketch[b] = part[b].astype(BF16)

    for p in range(held):
        store(p).wait()


def reduce_kernel(part, out_ref, *scratch):
    n = len(SPLIT)
    heard, held, got1, held2, got2, held3, got3 = (
        scratch[i * n : (i + 1) * n] for i in range(7)
    )
    send_sem, recv_sem = scratch[7 * n :]
    y, t = lax.axis_index("child"), lax.axis_index("tile")
    x, z, c = t // 8, lax.rem(t // 2, SIDE), lax.rem(t, 2)
    here = (y, x, z)

    def device(coords, core):
        return {"child": coords[0], "tile": coords[1] * 8 + coords[2] * 2 + core}

    def moved(axis, by):
        return tuple(shift(p, by) if a == axis else p for a, p in enumerate(here))

    sibling = device(here, 1 - c)
    greet([sibling] + [device(moved(a, by), c) for a in range(3) for by in (1, 2, 3)])

    await_greetings(10)

    pending = []

    def remote(src, dst, number, peer):
        copy = pltpu.make_async_remote_copy(
            src_ref=src,
            dst_ref=dst,
            send_sem=send_sem.at[number],
            recv_sem=recv_sem.at[number],
            device_id=peer,
        )
        pending.append(copy)
        copy.start()
        return copy

    swaps = [
        remote(part.at[:, :, :, 1 - c, pl.ds(at, rows)], heard[k], 9 * n + k, sibling)
        for k, (at, rows) in enumerate(SPLIT)
    ]

    def pick(ref, axis, which):
        return ref.at[(slice(None),) * axis + (which,)]

    def left_axes(k, stage):
        axes = [a for a in range(3) if a not in ORDERS[k][:stage]]
        return axes.index(ORDERS[k][stage])

    def scatter(k, stage, buf, got):
        axis, copies = ORDERS[k][stage], []
        at = left_axes(k, stage)
        for by in (2, 1, 3):
            copies.append(
                remote(
                    pick(buf, at, shift(here[axis], by)),
                    got.at[by - 1],
                    9 * k + 3 * stage + by - 1,
                    device(moved(axis, by), c),
                )
            )
        return copies

    def gather_up(k, stage, buf, got, copies, dst):
        axis = ORDERS[k][stage]
        for copy in copies:
            copy.wait_recv()
        kept = pick(buf, left_axes(k, stage), here[axis])[...].astype(F32)
        value = kept + got[0].astype(F32) + got[1].astype(F32) + got[2].astype(F32)
        dst[...] = value.astype(dst.dtype)

    flying = []
    for k, (at, rows) in enumerate(SPLIT):
        swaps[k].wait_recv()

        @pl.loop(0, SIDE)
        def _(a):
            mine = part[a, :, :, c, pl.ds(at, rows)].astype(F32)
            held[k][a] = (mine + heard[k][a].astype(F32)).astype(BF16)

        flying.append(scatter(k, 0, held[k], got1[k]))
    for k in range(n):
        gather_up(k, 0, held[k], got1[k], flying[k], held2[k])
        flying[k] = scatter(k, 1, held2[k], got2[k])
    for k in range(n):
        gather_up(k, 1, held2[k], got2[k], flying[k], held3[k])
        flying[k] = scatter(k, 2, held3[k], got3[k])
    for k, (at, rows) in enumerate(SPLIT):
        gather_up(k, 2, held3[k], got3[k], flying[k], out_ref.at[pl.ds(at, rows)])
    for copy in pending:
        copy.wait_send()


def shards(
    child_tiles,
    panel,
    bases,
    tile_blocks,
    tile_dest,
    tile_slot,
    parent_tiles,
    parent_blocks,
    sketch_test,
):
    owners = lax.axis_size("tile")
    _, count, order, _ = child_tiles.shape
    rank = bases.shape[2]
    width = sketch_test.shape[1]
    held = parent_tiles.shape[1]
    blocks = sketch_test.shape[0] // order
    chunk = sketch_test.shape[0] // (SIDE**3 * 2)
    hbm = pl.BlockSpec(memory_space=pltpu.HBM)
    smem = pl.BlockSpec(memory_space=pltpu.SMEM)
    vmem = pl.BlockSpec(memory_space=pltpu.VMEM)
    dma = pltpu.SemaphoreType.DMA

    shared, table = pl.pallas_call(
        functools.partial(route_kernel, owners),
        out_shape=(
            jax.ShapeDtypeStruct((SHARED, SIDE, 2, order, rank), BF16),
            jax.ShapeDtypeStruct((owners * CAP,), jnp.int32),
        ),
        in_specs=[smem, smem, smem, hbm, hbm, hbm],
        out_specs=(hbm, smem),
        scratch_shapes=[
            pltpu.VMEM((count, order, order), BF16),
            pltpu.VMEM((order, order), BF16),
            pltpu.VMEM((SIDE, SIDE, 2, order, rank), BF16),
            pltpu.VMEM((SIDE, SIDE, 2, rank, order), BF16),
            pltpu.VMEM((count, rank, rank), BF16),
            pltpu.VMEM((owners, CAP, rank, rank), BF16),
            pltpu.VMEM((owners, CAP, rank, rank), BF16),
            pltpu.VMEM((owners, CAP * rank, rank), BF16),
            dma((3,)),
            dma((2,)),
            dma((owners,)),
            dma((4, 24)),
            dma((4, 24)),
            dma((owners,)),
            dma((owners,)),
        ],
        compiler_params=pltpu.CompilerParams(
            collective_id=0, has_side_effects=True, vmem_limit_bytes=54 << 20
        ),
        name="encode_and_route",
    )(tile_blocks[0].T, tile_dest[0, :, 0], tile_slot[0], panel[0], bases[0], child_tiles[0])

    updated, part = pl.pallas_call(
        decode_kernel,
        out_shape=(
            jax.ShapeDtypeStruct((held, order, order), BF16),
            jax.ShapeDtypeStruct((blocks, order, width), BF16),
        ),
        in_specs=[smem, smem, hbm, hbm, hbm],
        out_specs=(hbm, vmem),
        scratch_shapes=[
            pltpu.VMEM((SIDE, SIDE, 2, order, rank), BF16),
            pltpu.VMEM((2, SIDE, 2, order, rank), BF16),
            pltpu.VMEM((held, order, order), BF16),
            pltpu.VMEM((blocks, order, width), BF16),
            pltpu.VMEM((order, order), F32),
            pltpu.VMEM((blocks, order, width), F32),
            pltpu.SMEM((held,), jnp.int32),
            pltpu.SMEM((held * owners * CAP,), jnp.int32),
            dma((3,)),
            dma((held,)),
            dma((held,)),
        ],
        compiler_params=pltpu.CompilerParams(vmem_limit_bytes=34 << 20),
        name="decode_and_sketch",
    )(
        table,
        parent_blocks[0].T,
        shared,
        parent_tiles[0],
        sketch_test.reshape(blocks, order, width),
    )

    def bufs(*lead):
        return [pltpu.VMEM((*lead, rows, width), BF16) for _, rows in SPLIT]

    row_sketch = pl.pallas_call(
        reduce_kernel,
        out_shape=jax.ShapeDtypeStruct((chunk, width), F32),
        in_specs=[vmem],
        out_specs=vmem,
        scratch_shapes=[
            *bufs(4, 4, 4),
            *bufs(4, 4, 4),
            *bufs(3, 4, 4),
            *bufs(4, 4),
            *bufs(3, 4),
            *bufs(4),
            *bufs(3),
            dma((10 * len(SPLIT),)),
            dma((10 * len(SPLIT),)),
        ],
        compiler_params=pltpu.CompilerParams(
            collective_id=1, has_side_effects=True, vmem_limit_bytes=32 << 20
        ),
        name="reduce_sketch",
    )(part.reshape(SIDE, SIDE, SIDE, 2, chunk, width))
    return (updated[None], row_sketch)


def solution(mesh):
    return jax.shard_map(
        shards,
        mesh=mesh,
        in_specs=(
            P("child", "tile", None, None),
            P("child", "tile", None),
            P("child", "tile", None),
            P("child", None, None),
            P("child", None, None),
            P("child", None),
            P("child", "tile", None, None),
            P("child", "tile", None),
            P(),
        ),
        out_specs=(P("child", "tile", None, None), P(("child", "tile"), None)),
        check_vma=False,
    )
```

```python
import functools

import jax
import jax.numpy as jnp
from jax import lax
from jax.experimental import pallas as pl
from jax.experimental.pallas import tpu as pltpu
from jax.sharding import PartitionSpec as P

CAP = 2
SIDE = 4
F32 = jnp.float32
BF16 = jnp.bfloat16
PLAN = (
    (0, 0), (0, 1), (5, 0), (0, 2), (0, 3), (0, 4), (0, 5), (0, 6), (1, 0), (1, 1), (0, 7), (0, 8),
    (0, 9), (0, 10), (0, 11), (1, 2), (1, 3), (0, 12), (0, 13), (0, 14), (0, 15), (1, 4),
    (2, 0), (1, 5), (2, 1), (1, 6), (2, 2), (1, 7), (2, 3), (1, 8),
    (3, 0), (1, 9), (3, 1), (1, 10), (3, 2), (1, 11), (3, 3), (4, 0), (1, 12), (1, 13), (1, 14), (1, 15),
)
SHARED = 40
SPLIT = ((0, 32), (32, 32), (64, 16), (80, 16), (96, 16), (112, 16))
ORDERS = ((0, 1, 2), (1, 2, 0), (2, 0, 1)) * 2


def dot(a, b, ca, cb):
    return lax.dot_general(a, b, (((ca,), (cb,)), ((), ())), preferred_element_type=F32)


def shift(p, by):
    return lax.rem(p + by + SIDE, SIDE)


def greet(devices):
    barrier = pltpu.get_barrier_semaphore()
    for device in devices:
        pl.semaphore_signal(barrier, inc=1, device_id=device)


def await_greetings(count):
    pl.semaphore_wait(pltpu.get_barrier_semaphore(), count)


def route_kernel(
    owners,
    blocks_ref,
    dest_ref,
    slot_ref,
    panel_hbm,
    bases_hbm,
    tiles_hbm,
    shared,
    table_ref,
    tiles,
    panel,
    bases,
    proj,
    cores,
    outgoing,
    incoming,
    settled,
    load_sem,
    own_sem,
    keep_sem,
    send_sem,
    recv_sem,
    a2a_send,
    a2a_recv,
):
    t = lax.axis_index("tile")
    x, z, c = t // 8, lax.rem(t // 2, SIDE), lax.rem(t, 2)
    count, rank = tiles.shape[0], cores.shape[1]

    load_panel = pltpu.make_async_copy(panel_hbm, panel, load_sem.at[0])
    load_bases = pltpu.make_async_copy(bases_hbm, bases.at[x, z, c], load_sem.at[1])
    load_tiles = pltpu.make_async_copy(tiles_hbm, tiles, load_sem.at[2])
    load_bases.start()
    load_panel.start()
    load_tiles.start()

    @pl.loop(1, owners)
    def _(step):
        pl.semaphore_signal(
            pltpu.get_barrier_semaphore(),
            inc=1,
            device_id={"tile": lax.rem(t + step, owners)},
        )

    load_bases.wait()
    await_greetings(owners - 1)

    sibling = t + 1 - 2 * c
    pending = []

    class Gather:
        offsets = (None, 0, -1, 1, 2)

        def __init__(self, number, buf, x_first):
            self.n, self.buf, self.x_first = number, buf, x_first
            self.f, self.s = (x, z) if x_first else (z, x)
            self.rows = buf.shape[3] // 2
            self.start = 0 if x_first else self.rows

        def at(self, first, second, core, at=0, rows=None):
            place = (first, second) if self.x_first else (second, first)
            return self.buf.at[(*place, core, pl.ds(self.start + at, rows or self.rows))]

        def place(self, ring, by):
            if ring == 0:
                return shift(self.f, by), self.s
            return shift(self.f, self.offsets[ring]), shift(self.s, by)

        def peer(self, ring, by):
            first, second = (self.f, shift(self.s, by)) if ring else self.place(0, by)
            return (first if self.x_first else second) * 8 + (second if self.x_first else first) * 2 + c

        def copy(self, ref, peer, k):
            return pltpu.make_async_remote_copy(
                src_ref=ref,
                dst_ref=ref,
                send_sem=send_sem.at[self.n, k],
                recv_sem=recv_sem.at[self.n, k],
                device_id={"tile": peer},
            )

        def send(self, ref, peer, k):
            copy = self.copy(ref, peer, k)
            copy.start()
            pending.append(copy)

        def block(self, ring, by, half=None):
            if half is None:
                return self.at(*self.place(ring, by), c)
            return self.at(*self.place(ring, by), c, half * (self.rows // 2), self.rows // 2)

        def open(self, ring):
            for k, by in enumerate((1, -1) if ring else (1, -1, 2)):
                self.send(self.block(ring, 0), self.peer(ring, by), 4 * ring + k)

        def relay(self, ring):
            for k, by in enumerate((-1, 1)):
                self.copy(self.block(ring, by), self.peer(ring, by), 4 * ring + k).wait_recv()
                if ring:
                    self.send(self.block(ring, by, k), self.peer(ring, -by), 4 * ring + 2 + k)
                else:
                    self.open(2 + k)

        def close(self, ring):
            if ring == 0:
                self.copy(self.block(0, 2), self.peer(0, 2), 2).wait_recv()
                self.open(4)
                return
            for k, by in enumerate((-1, 1)):
                self.copy(self.block(ring, 2, k), self.peer(ring, by), 4 * ring + 2 + k).wait_recv()
            self.send(self.line(ring, c), sibling, 19 + ring)

        def line(self, ring, core):
            return self.at(self.place(ring, 0)[0], slice(None), core)

        def from_sibling(self, ring):
            self.copy(self.line(ring, 1 - c), sibling, 19 + ring).wait_recv()

    def of(buf, which, tile):
        block = blocks_ref[which, tile]
        return buf[block >> 3, (block >> 1) & 3, block & 1]

    def encode(start, stop):
        @pl.loop(start, stop, unroll=4)
        def _(q):
            tile = t * count + q
            half = dot(of(bases, 0, tile), tiles[q], 0, 0).astype(BF16)
            cores[q] = dot(half, of(bases, 1, tile), 1, 0).astype(BF16)

    steps = (
        ("open", 0), ("open", 1), ("relay", 0), ("relay", 1), ("close", 0), ("relay", 2),
        ("relay", 3), ("close", 1), ("relay", 4), ("close", 2), ("close", 3), ("close", 4),
        ("from_sibling", 1), ("from_sibling", 2), ("from_sibling", 3), ("from_sibling", 4),
    )
    arrays = (
        (Gather(0, bases, True), Gather(1, bases, False)),
        (Gather(2, proj, True), Gather(3, proj, False)),
    )
    dests = [dest_ref[t * count + q] for q in range(count)]

    def partner(step, sign):
        off = lax.rem(step * 11, owners)
        dx, dz, dc = off // 8, lax.rem(off // 2, SIDE), lax.rem(off, 2)
        px, pz, pc = shift(x, sign * dx), shift(z, sign * dz), lax.rem(c + dc, 2)
        return px * 8 + pz * 2 + pc

    def outbound(step, source, target):
        return pltpu.make_async_remote_copy(
            src_ref=outgoing.at[step],
            dst_ref=incoming.at[source],
            send_sem=a2a_send.at[step],
            recv_sem=a2a_recv.at[step],
            device_id={"tile": target},
        )

    def pack(step, target):
        first, last = jnp.int32(0), jnp.int32(0)
        for q in range(count):
            last = jnp.where(dests[q] == target, q, last)
            back = count - 1 - q
            first = jnp.where(dests[back] == target, back, first)
        outgoing[step, 0] = cores[first]
        outgoing[step, 1] = cores[last]

    def dispatch(start, stop):
        @pl.loop(max(start, 1), stop)
        def _(step):
            target = partner(step, 1)
            pack(step, target)
            outbound(step, t, target).start()

    def foretell():
        @pl.loop(0, owners)
        def _(source):
            first, last, found = jnp.int32(0), jnp.int32(0), jnp.int32(0)
            for q in range(count):
                tile = source * count + q
                hit = dest_ref[tile] == t
                last = jnp.where(hit, tile, last)
                first = jnp.where(hit & (found == 0), tile, first)
                found = found + hit.astype(jnp.int32)
            for k, tile in enumerate((first, last)):
                entry = blocks_ref[0, tile] + blocks_ref[1, tile] * 256 + slot_ref[tile] * 65536
                table_ref[source * CAP + k] = jnp.where(found > k, entry, -1)

    each, wave = count // 4, owners // 4
    for what, at in PLAN:
        if what == 2:
            if at == 0:
                keep_bases = pltpu.make_async_copy(bases, shared.at[pl.ds(0, SIDE)], own_sem.at[1])
                keep_bases.start()
                load_tiles.wait()
            encode(at * each, at * each + each)
        elif what == 3:
            dispatch(at * wave, at * wave + wave)
        elif what == 4:
            foretell()
        elif what == 5:
            load_panel.wait()
            proj[x, z, c] = dot(bases[x, z, c], panel[...], 0, 0).astype(BF16)
        else:
            step, ring = steps[at]
            for gather in arrays[what]:
                getattr(gather, step)(ring)

    def keep(source):
        place = (source // 16, lax.rem(source // 4, SIDE), lax.rem(source // 2, 2))
        rows = pl.ds(pl.multiple_of(lax.rem(source, 2) * CAP * rank, CAP * rank), CAP * rank)
        return pltpu.make_async_copy(
            settled.at[source],
            shared.at[SIDE + place[0], place[1], place[2], rows],
            keep_sem.at[source],
        )

    def settle(source, received):
        for k in range(CAP):
            entry = jnp.maximum(table_ref[source * CAP + k], 0)
            i, j = entry & 255, (entry >> 8) & 255
            cross = dot(
                proj[i >> 3, (i >> 1) & 3, i & 1], proj[j >> 3, (j >> 1) & 3, j & 1], 1, 1
            )
            core = received[k].astype(F32) - cross
            settled[source, k * rank : (k + 1) * rank] = core.astype(BF16)
        keep(source).start()

    pack(0, t)
    settle(t, outgoing.at[0])

    @pl.loop(1, owners)
    def _(step):
        source = partner(step, -1)
        outbound(step, source, source).wait()
        settle(source, incoming.at[source])

    @pl.loop(0, owners)
    def _(source):
        keep(source).wait()

    keep_bases.wait()
    for copy in pending:
        copy.wait_send()


def decode_kernel(
    table_ref,
    pblocks_ref,
    shared,
    parents_hbm,
    test_hbm,
    updated_hbm,
    sketch,
    bases,
    cores,
    parents,
    test,
    total,
    part,
    number_of,
    listed,
    touched,
    load_sem,
    tile_sem,
    store_sem,
):
    held = parents.shape[0]
    blocks, places = part.shape[0], table_ref.shape[0]
    rank = cores.shape[4]

    def load(p):
        return pltpu.make_async_copy(parents_hbm.at[p], parents.at[p], tile_sem.at[p])

    def store(p):
        return pltpu.make_async_copy(parents.at[p], updated_hbm.at[p], store_sem.at[p])

    load_cores = pltpu.make_async_copy(shared.at[pl.ds(SIDE, 2)], cores, load_sem.at[0])
    load_bases = pltpu.make_async_copy(shared.at[pl.ds(0, SIDE)], bases, load_sem.at[1])
    load_test = pltpu.make_async_copy(test_hbm, test, load_sem.at[2])
    load_cores.start()
    load_bases.start()
    for p in range(held):
        load(p).start()
    load_test.start()

    @pl.loop(0, blocks)
    def _(b):
        sketch[b] = jnp.zeros_like(sketch[b])
        touched[b] = 0

    for p in range(held):
        number_of[p] = 0

    @pl.loop(0, places)
    def _(k):
        entry = table_ref[k]

        @pl.when(entry >= 0)
        def _():
            slot = entry >> 16
            n = number_of[slot]
            listed[slot * places + n] = k
            number_of[slot] = n + 1

    def basis(block):
        return bases[block >> 3, (block >> 1) & 3, block & 1]

    def core(k):
        rows = pl.ds(pl.multiple_of((k & 3) * rank, rank), rank)
        return cores[k >> 5, (k >> 3) & 3, (k >> 2) & 1, rows]

    def accumulate(block, value):
        seen = touched[block]

        @pl.when(seen == 0)
        def _():
            part[block] = value

        @pl.when(seen > 0)
        def _():
            part[block] += value

        touched[block] = 1

    empty = jnp.zeros((rank, rank), BF16)
    load_cores.wait()
    load_bases.wait()
    load_test.wait()

    @pl.loop(0, held)
    def _(p):
        load(p).wait()
        total[...] = parents[p].astype(F32)
        n = number_of[p]

        def add(at, wide):
            lefts, rights = [], []
            for pair in range(0, wide, 2):
                rows, cols, middle = [], [], []
                for one in (at + pair, at + pair + 1):
                    k = listed[p * places + jnp.minimum(one, n - 1)]
                    entry = table_ref[k]
                    rows.append(basis(entry & 255))
                    cols.append(basis((entry >> 8) & 255))
                    middle.append(jnp.where(one < n, core(k), empty))
                block = jnp.concatenate(
                    [
                        jnp.concatenate([middle[0], empty], axis=1),
                        jnp.concatenate([empty, middle[1]], axis=1),
                    ],
                    axis=0,
                )
                left = dot(jnp.concatenate(rows, axis=1), block, 1, 0)
                lefts.append(left.astype(BF16))
                rights += cols
            left = jnp.concatenate(lefts, axis=1)
            total[...] += dot(left, jnp.concatenate(rights, axis=1), 1, 1)

        eights = (n + 3) // 8

        @pl.loop(0, eights)
        def _(m):
            add(8 * m, 8)

        rest = jnp.maximum(n - 8 * eights, 0)
        fours = (rest + 1) // 4

        @pl.loop(0, fours)
        def _(m):
            add(8 * eights + 4 * m, 4)

        @pl.when(4 * fours < rest)
        def _():
            add(8 * eights + 4 * fours, 2)

        new = total[...].astype(BF16)
        parents[p] = new
        store(p).start()
        a, b = pblocks_ref[0, p], pblocks_ref[1, p]
        accumulate(a, dot(new, test[b], 1, 0))

        @pl.when(a != b)
        def _():
            accumulate(b, dot(new, test[a], 0, 0))

    @pl.loop(0, blocks)
    def _(b):
        @pl.when(touched[b] > 0)
        def _():
            sketch[b] = part[b].astype(BF16)

    for p in range(held):
        store(p).wait()


def reduce_kernel(part, out_ref, *scratch):
    n = len(SPLIT)
    heard, held, got1, held2, got2, held3, got3 = (
        scratch[i * n : (i + 1) * n] for i in range(7)
    )
    send_sem, recv_sem = scratch[7 * n :]
    y, t = lax.axis_index("child"), lax.axis_index("tile")
    x, z, c = t // 8, lax.rem(t // 2, SIDE), lax.rem(t, 2)
    here = (y, x, z)

    def device(coords, core):
        return {"child": coords[0], "tile": coords[1] * 8 + coords[2] * 2 + core}

    def moved(axis, by):
        return tuple(shift(p, by) if a == axis else p for a, p in enumerate(here))

    sibling = device(here, 1 - c)
    greet([sibling] + [device(moved(a, by), c) for a in range(3) for by in (1, 2, 3)])

    await_greetings(10)

    pending = []

    def remote(src, dst, number, peer):
        copy = pltpu.make_async_remote_copy(
            src_ref=src,
            dst_ref=dst,
            send_sem=send_sem.at[number],
            recv_sem=recv_sem.at[number],
            device_id=peer,
        )
        pending.append(copy)
        copy.start()
        return copy

    swaps = [
        remote(part.at[:, :, :, 1 - c, pl.ds(at, rows)], heard[k], 9 * n + k, sibling)
        for k, (at, rows) in enumerate(SPLIT)
    ]

    def pick(ref, axis, which):
        return ref.at[(slice(None),) * axis + (which,)]

    def left_axes(k, stage):
        axes = [a for a in range(3) if a not in ORDERS[k][:stage]]
        return axes.index(ORDERS[k][stage])

    def scatter(k, stage, buf, got):
        axis, copies = ORDERS[k][stage], []
        at = left_axes(k, stage)
        for by in (2, 1, 3):
            copies.append(
                remote(
                    pick(buf, at, shift(here[axis], by)),
                    got.at[by - 1],
                    9 * k + 3 * stage + by - 1,
                    device(moved(axis, by), c),
                )
            )
        return copies

    def gather_up(k, stage, buf, got, copies, dst):
        axis = ORDERS[k][stage]
        for copy in copies:
            copy.wait_recv()
        kept = pick(buf, left_axes(k, stage), here[axis])[...].astype(F32)
        value = kept + got[0].astype(F32) + got[1].astype(F32) + got[2].astype(F32)
        dst[...] = value.astype(dst.dtype)

    flying = []
    for k, (at, rows) in enumerate(SPLIT):
        swaps[k].wait_recv()

        @pl.loop(0, SIDE)
        def _(a):
            mine = part[a, :, :, c, pl.ds(at, rows)].astype(F32)
            held[k][a] = (mine + heard[k][a].astype(F32)).astype(BF16)

        flying.append(scatter(k, 0, held[k], got1[k]))
    for k in range(n):
        gather_up(k, 0, held[k], got1[k], flying[k], held2[k])
        flying[k] = scatter(k, 1, held2[k], got2[k])
    for k in range(n):
        gather_up(k, 1, held2[k], got2[k], flying[k], held3[k])
        flying[k] = scatter(k, 2, held3[k], got3[k])
    for k, (at, rows) in enumerate(SPLIT):
        gather_up(k, 2, held3[k], got3[k], flying[k], out_ref.at[pl.ds(at, rows)])
    for copy in pending:
        copy.wait_send()


def shards(
    child_tiles,
    panel,
    bases,
    tile_blocks,
    tile_dest,
    tile_slot,
    parent_tiles,
    parent_blocks,
    sketch_test,
):
    owners = lax.axis_size("tile")
    _, count, order, _ = child_tiles.shape
    rank = bases.shape[2]
    width = sketch_test.shape[1]
    held = parent_tiles.shape[1]
    blocks = sketch_test.shape[0] // order
    chunk = sketch_test.shape[0] // (SIDE**3 * 2)
    hbm = pl.BlockSpec(memory_space=pltpu.HBM)
    smem = pl.BlockSpec(memory_space=pltpu.SMEM)
    vmem = pl.BlockSpec(memory_space=pltpu.VMEM)
    dma = pltpu.SemaphoreType.DMA

    shared, table = pl.pallas_call(
        functools.partial(route_kernel, owners),
        out_shape=(
            jax.ShapeDtypeStruct((SHARED, SIDE, 2, order, rank), BF16),
            jax.ShapeDtypeStruct((owners * CAP,), jnp.int32),
        ),
        in_specs=[smem, smem, smem, hbm, hbm, hbm],
        out_specs=(hbm, smem),
        scratch_shapes=[
            pltpu.VMEM((count, order, order), BF16),
            pltpu.VMEM((order, order), BF16),
            pltpu.VMEM((SIDE, SIDE, 2, order, rank), BF16),
            pltpu.VMEM((SIDE, SIDE, 2, rank, order), BF16),
            pltpu.VMEM((count, rank, rank), BF16),
            pltpu.VMEM((owners, CAP, rank, rank), BF16),
            pltpu.VMEM((owners, CAP, rank, rank), BF16),
            pltpu.VMEM((owners, CAP * rank, rank), BF16),
            dma((3,)),
            dma((2,)),
            dma((owners,)),
            dma((4, 24)),
            dma((4, 24)),
            dma((owners,)),
            dma((owners,)),
        ],
        compiler_params=pltpu.CompilerParams(
            collective_id=0, has_side_effects=True, vmem_limit_bytes=54 << 20
        ),
        name="encode_and_route",
    )(tile_blocks[0].T, tile_dest[0, :, 0], tile_slot[0], panel[0], bases[0], child_tiles[0])

    updated, part = pl.pallas_call(
        decode_kernel,
        out_shape=(
            jax.ShapeDtypeStruct((held, order, order), BF16),
            jax.ShapeDtypeStruct((blocks, order, width), BF16),
        ),
        in_specs=[smem, smem, hbm, hbm, hbm],
        out_specs=(hbm, vmem),
        scratch_shapes=[
            pltpu.VMEM((SIDE, SIDE, 2, order, rank), BF16),
            pltpu.VMEM((2, SIDE, 2, order, rank), BF16),
            pltpu.VMEM((held, order, order), BF16),
            pltpu.VMEM((blocks, order, width), BF16),
            pltpu.VMEM((order, order), F32),
            pltpu.VMEM((blocks, order, width), F32),
            pltpu.SMEM((held,), jnp.int32),
            pltpu.SMEM((held * owners * CAP,), jnp.int32),
            pltpu.SMEM((blocks,), jnp.int32),
            dma((3,)),
            dma((held,)),
            dma((held,)),
        ],
        compiler_params=pltpu.CompilerParams(vmem_limit_bytes=34 << 20),
        name="decode_and_sketch",
    )(
        table,
        parent_blocks[0].T,
        shared,
        parent_tiles[0],
        sketch_test.reshape(blocks, order, width),
    )

    def bufs(*lead):
        return [pltpu.VMEM((*lead, rows, width), BF16) for _, rows in SPLIT]

    row_sketch = pl.pallas_call(
        reduce_kernel,
        out_shape=jax.ShapeDtypeStruct((chunk, width), F32),
        in_specs=[vmem],
        out_specs=vmem,
        scratch_shapes=[
            *bufs(4, 4, 4),
            *bufs(4, 4, 4),
            *bufs(3, 4, 4),
            *bufs(4, 4),
            *bufs(3, 4),
            *bufs(4),
            *bufs(3),
            dma((10 * len(SPLIT),)),
            dma((10 * len(SPLIT),)),
        ],
        compiler_params=pltpu.CompilerParams(
            collective_id=1, has_side_effects=True, vmem_limit_bytes=32 << 20
        ),
        name="reduce_sketch",
    )(part.reshape(SIDE, SIDE, SIDE, 2, chunk, width))
    return (updated[None], row_sketch)


def solution(mesh):
    return jax.shard_map(
        shards,
        mesh=mesh,
        in_specs=(
            P("child", "tile", None, None),
            P("child", "tile", None),
            P("child", "tile", None),
            P("child", None, None),
            P("child", None, None),
            P("child", None),
            P("child", "tile", None, None),
            P("child", "tile", None),
            P(),
        ),
        out_specs=(P("child", "tile", None, None), P(("child", "tile"), None)),
        check_vma=False,
    )
```
